512 devices in a mesh: sims: 32 (over z_lo, y, core), sites: 16 (over x, z_hi).
Axes of the slice: x: 4, y: 8, z: 8 (z_hi: 4, z_lo: 2; z = z_hi * 2 + z_lo), core: 2. Of those that a mesh axis runs over, the one named last changes fastest.
Arguments:
- genotypes: int32 [32, 64, 8192], P('sims', None, 'sites'), may hold values from 0 to 1
- key_prior: bfloat16 [32, 2048], P('sims', 'sites'), may hold values from -300 to 300
- band_reach: int32 [32], P('sims'), may hold values from 128 to 512, as said below
- cotangent: bfloat16 [32, 2048, 512], P('sims', 'sites'), may hold values from -0.09375 to 0.09375
- conv_weight: float32 [4, 64], replicated, may hold values from -3 to 3
- conv_bias: float32 [64], replicated, may hold values from -3 to 3
- mix_weight: float32 [3, 64, 64], replicated, may hold values from -0.4375 to 0.4375
- embed_weight: float32 [64, 512], replicated, may hold values from -0.75 to 0.75
- norm_gain: float32 [512], replicated, may hold values from 0.5 to 1.5
- attn_weight: bfloat16 [4, 512, 512], replicated, may hold values from -0.25 to 0.25
Outputs:
- grad_attention: float32 [1048576], P(('sims', 'sites'))
- grad_conv: float32 [4, 64], replicated
- grad_bias: float32 [64], replicated
- grad_mix: float32 [3, 64, 64], replicated
- grad_embed: float32 [64, 512], replicated
- grad_gain: float32 [512], replicated
The draws below stay inside these ranges and needn't reach their ends.
Inputs may be any that keep to these rules, and one draw needn't show every extreme that they name: `band_reach`: some evolution has reach exactly 512 in every draw.
All inputs are finite; a program needn't handle non-finite values.
Results may differ from the reference program's by a relative error of at most 0.017.
Values may be sent and summed in bfloat16 or wider, within the bound.
A program may use at most 64 MiB of HBM per device.

```python
import math
import jax
import jax.numpy as jnp
from jax import lax

D = 512
HEADS = 8
HEAD_DIM = 64
CH = 64
HAPS = 64
PATCH = 4
BAND = 512
SIMS = 32
TOKENS = 2048
SITES = 8192


def draw_genotypes(key, part):
    base = jax.random.fold_in(key, 101)
    level_key, cell_key = jax.random.split(base)
    levels = jax.random.randint(level_key, (SIMS, 1, SITES), 1, 16)
    cells = jax.random.randint(cell_key, (SIMS, HAPS, SITES), 0, 16)
    return (cells < levels).astype(jnp.int32)


def draw_band_reach(key, part):
    base = jax.random.fold_in(key, 202)
    value_key, place_key = jax.random.split(base)
    drawn = jax.random.randint(value_key, (SIMS,), BAND // 4, BAND + 1)
    chosen = jax.random.randint(place_key, (), 0, SIMS)
    return jnp.where(jnp.arange(SIMS) == chosen, BAND, drawn).astype(jnp.int32)


def draw_key_prior(key, part):
    base = jax.random.fold_in(key, 303)
    value_key = jax.random.fold_in(base, 0)
    values = jnp.clip(jax.random.normal(value_key, (SIMS, TOKENS), jnp.float32), -4.0, 4.0)
    return values.astype(jnp.bfloat16)


def level_of(key, dims, pieces, least, high):
    def one(dim, parts):
        steps = jax.random.uniform(jax.random.fold_in(jax.random.fold_in(key, 6), dim), (parts,), jnp.float32, least / len(pieces), high / len(pieces))
        return jnp.repeat(jnp.exp(steps), dims[dim] // parts).reshape((-1,) + (1,) * (len(dims) - dim - 1))

    gain = one(*pieces[0])
    for cut in pieces[1:]:
        gain = gain * one(*cut)
    return gain


def gaussian(own_key, extent, width, bound, shards=(), kind=jnp.bfloat16):
    gain = level_of(own_key, extent, shards, -0.22, 0.18) if shards else 1.0
    values = jax.random.normal(own_key, extent, jnp.float32) * width * gain
    return jnp.minimum(jnp.maximum(values, -bound), bound).astype(kind)


def setup_inputs(seed: int = 0) -> dict:
    arg_keys = jax.random.split(jax.random.key(seed), 11)
    genotypes = draw_genotypes(jax.random.fold_in(arg_keys[10], 71), 0)
    key_prior = draw_key_prior(jax.random.fold_in(arg_keys[10], 71), 0)
    band_reach = draw_band_reach(jax.random.fold_in(arg_keys[10], 71), 0)
    cotangent = gaussian(arg_keys[3], (SIMS, TOKENS, D), (4.0 * (SIMS * TOKENS) ** -0.5), 0.09375, ((0, 32), (1, 16)))
    conv_weight = gaussian(arg_keys[4], (PATCH, CH), PATCH ** -0.5, 3.0, (), jnp.float32)
    conv_bias = gaussian(arg_keys[5], (CH,), 0.5, 3.0, (), jnp.float32)
    mix_weight = gaussian(arg_keys[6], (3, CH, CH), (3 * CH) ** -0.5, 0.4375, (), jnp.float32)
    embed_weight = gaussian(arg_keys[7], (CH, D), CH ** -0.5, 0.75, (), jnp.float32)
    norm_gain = jnp.clip(1.0 + 0.1 * jax.random.normal(arg_keys[8], (D,), jnp.float32), 0.5, 1.5)
    attn_weight = gaussian(arg_keys[9], (4, D, D), D ** -0.5, 0.25)
    return {"genotypes": genotypes, "key_prior": key_prior, "band_reach": band_reach, "cotangent": cotangent, "conv_weight": conv_weight, "conv_bias": conv_bias, "mix_weight": mix_weight, "embed_weight": embed_weight, "norm_gain": norm_gain, "attn_weight": attn_weight}


HIGH = lax.Precision.HIGHEST
EPS = 1e-06

def silu_slope(value):
    sigma = jax.nn.sigmoid(value)
    return sigma * (1.0 + value * (1.0 - sigma))

def one_sim(genotype, prior, limit, upstream, conv_weight, conv_bias, mix_weight, embed_weight, norm_gain, attn_weight):
    patches = genotype.astype(jnp.float32).reshape(HAPS, TOKENS, PATCH)
    pre = jnp.einsum('htk,kc->hct', patches, conv_weight, precision=HIGH) + conv_bias[None, :, None]
    pooled = lax.optimization_barrier(jnp.mean(jax.nn.silu(pre), axis=0))
    mixed = jnp.zeros((CH, TOKENS), jnp.float32)
    for shift_by in (-1, 0, 1):
        mixed = mixed + jnp.einsum('co,ct->ot', mix_weight[shift_by + 1], jnp.roll(pooled, -shift_by, axis=1), precision=HIGH)
    activated = jax.nn.silu(mixed)
    embedded = jnp.einsum('ct,cd->td', activated, embed_weight, precision=HIGH).astype(jnp.bfloat16)
    wide = embedded.astype(jnp.float32)
    inverse = lax.rsqrt(lax.optimization_barrier(jnp.mean(wide * wide, axis=1, keepdims=True)) + EPS)
    normed = (wide * inverse * norm_gain).astype(jnp.bfloat16)
    query = jnp.dot(normed, attn_weight[0], preferred_element_type=jnp.float32).astype(jnp.bfloat16)
    keys = jnp.dot(normed, attn_weight[1], preferred_element_type=jnp.float32).astype(jnp.bfloat16)
    values = jnp.dot(normed, attn_weight[2], preferred_element_type=jnp.float32).astype(jnp.bfloat16)
    grad_attended = jnp.dot(upstream, attn_weight[3].T, preferred_element_type=jnp.float32).astype(jnp.bfloat16)
    query_heads = query.reshape(TOKENS, HEADS, HEAD_DIM)
    key_heads = keys.reshape(TOKENS, HEADS, HEAD_DIM)
    value_heads = values.reshape(TOKENS, HEADS, HEAD_DIM)
    grad_heads = grad_attended.reshape(TOKENS, HEADS, HEAD_DIM)
    factor = HEAD_DIM ** (-0.5)
    block_rows = math.gcd(512, TOKENS)
    span = block_rows + 2 * BAND
    full_keys = span >= TOKENS
    positions = jnp.arange(TOKENS, dtype=jnp.int32)
    prior_wide = prior.astype(jnp.float32)

    def visit(carry, start):
        key_grad, value_grad = carry
        rows = start + jnp.arange(block_rows, dtype=jnp.int32)
        if full_keys:
            columns = positions
        else:
            columns = ((start - BAND + jnp.arange(span, dtype=jnp.int32)) % TOKENS).astype(jnp.int32)
        block_query = lax.dynamic_slice_in_dim(query_heads, start, block_rows, 0).astype(jnp.float32)
        block_grad = lax.dynamic_slice_in_dim(grad_heads, start, block_rows, 0).astype(jnp.float32)
        block_keys = key_heads[columns].astype(jnp.float32)
        block_values = value_heads[columns].astype(jnp.float32)
        scores = jnp.einsum('qhe,khe->hqk', block_query, block_keys) * factor
        scores = scores + prior_wide[columns][None, None, :]
        apart = (columns[None, :] - rows[:, None]) % TOKENS
        apart = jnp.minimum(apart, TOKENS - apart)
        inside = (apart <= limit)[None]
        row_top = lax.optimization_barrier(jnp.max(jnp.where(inside, scores, -jnp.inf), axis=-1, keepdims=True))
        lifted = jnp.where(inside, jnp.exp(scores - row_top), 0.0)
        row_total = lax.optimization_barrier(jnp.sum(lifted, axis=-1, keepdims=True))
        prob = lifted / row_total
        prob_half = prob.astype(jnp.bfloat16).astype(jnp.float32)
        attended_full = jnp.einsum('hqk,khe->qhe', prob_half, block_values)
        delta = jnp.einsum('qhe,qhe->hq', block_grad, attended_full)
        grad_prob = jnp.einsum('qhe,khe->hqk', block_grad, block_values)
        grad_scores = (prob * (grad_prob - delta[..., None]) * factor).astype(jnp.bfloat16).astype(jnp.float32)
        grad_query = jnp.einsum('hqk,khe->qhe', grad_scores, block_keys).astype(jnp.bfloat16)
        key_grad = key_grad.at[columns].add(jnp.einsum('hqk,qhe->khe', grad_scores, block_query))
        value_grad = value_grad.at[columns].add(jnp.einsum('hqk,qhe->khe', prob_half, block_grad))
        return ((key_grad, value_grad), (attended_full.astype(jnp.bfloat16), grad_query))
    starts = (jnp.arange(TOKENS // block_rows, dtype=jnp.int32) * block_rows).astype(jnp.int32)
    zero_heads = jnp.zeros((TOKENS, HEADS, HEAD_DIM), jnp.float32)
    (key_grad, value_grad), (attended_blocks, query_blocks) = lax.scan(visit, (zero_heads, zero_heads), starts)
    attended = attended_blocks.reshape(TOKENS, D)
    grad_query = query_blocks.reshape(TOKENS, D)
    grad_keys = key_grad.astype(jnp.bfloat16).reshape(TOKENS, D)
    grad_values = value_grad.astype(jnp.bfloat16).reshape(TOKENS, D)
    term_query = jnp.dot(normed.T, grad_query, preferred_element_type=jnp.float32)
    term_keys = jnp.dot(normed.T, grad_keys, preferred_element_type=jnp.float32)
    term_values = jnp.dot(normed.T, grad_values, preferred_element_type=jnp.float32)
    term_output = jnp.dot(attended.T, upstream, preferred_element_type=jnp.float32)
    grad_normed = jnp.dot(grad_query, attn_weight[0].T, preferred_element_type=jnp.float32)
    grad_normed = grad_normed + jnp.dot(grad_keys, attn_weight[1].T, preferred_element_type=jnp.float32)
    grad_normed = grad_normed + jnp.dot(grad_values, attn_weight[2].T, preferred_element_type=jnp.float32)
    term_gain = lax.optimization_barrier(jnp.sum(grad_normed * wide * inverse, axis=0))
    scaled = grad_normed * norm_gain
    grad_embedded = inverse * scaled - wide * inverse ** 3 * lax.optimization_barrier(jnp.sum(scaled * wide, axis=1, keepdims=True)) / D
    grad_embedded = grad_embedded + upstream.astype(jnp.float32)
    term_embed = jnp.einsum('ct,td->cd', activated, grad_embedded, precision=HIGH)
    grad_mixed = jnp.einsum('td,od->ot', grad_embedded, embed_weight, precision=HIGH) * silu_slope(mixed)
    mix_terms = []
    grad_pooled = jnp.zeros((CH, TOKENS), jnp.float32)
    for shift_by in (-1, 0, 1):
        mix_terms.append(jnp.einsum('ct,ot->co', jnp.roll(pooled, -shift_by, axis=1), grad_mixed, precision=HIGH))
        grad_pooled = grad_pooled + jnp.roll(jnp.einsum('co,ot->ct', mix_weight[shift_by + 1], grad_mixed, precision=HIGH), shift_by, axis=1)
    grad_pre = (grad_pooled / HAPS)[None] * silu_slope(pre)
    term_conv = jnp.einsum('htk,hct->kc', patches, grad_pre, precision=HIGH)
    term_bias = lax.optimization_barrier(jnp.sum(grad_pre, axis=(0, 2)))
    return (term_query, term_keys, term_values, term_output, term_conv, term_bias, jnp.stack(mix_terms), term_embed, term_gain)

def reference(genotypes, key_prior, band_reach, cotangent, conv_weight, conv_bias, mix_weight, embed_weight, norm_gain, attn_weight):

    def add_sim(totals, inputs):
        genotype, prior, limit, upstream = inputs
        terms = one_sim(genotype, prior, limit, upstream, conv_weight, conv_bias, mix_weight, embed_weight, norm_gain, attn_weight)
        return (jax.tree.map(jnp.add, totals, terms), None)
    square = jnp.zeros((D, D), jnp.float32)
    start_totals = (square, square, square, square, jnp.zeros((PATCH, CH), jnp.float32), jnp.zeros((CH,), jnp.float32), jnp.zeros((3, CH, CH), jnp.float32), jnp.zeros((CH, D), jnp.float32), jnp.zeros((D,), jnp.float32))
    totals, unused = lax.scan(add_sim, start_totals, (genotypes, key_prior, band_reach, cotangent))
    grad_attention = jnp.stack([totals[0], totals[1], totals[2], totals[3]]).reshape(-1)
    return (grad_attention, totals[4], totals[5], totals[6], totals[7], totals[8])
```

```python
import jax
import jax.numpy as jnp
from jax import lax
from jax.sharding import PartitionSpec as P

HEADS = 8
HEAD_DIM = 64
BAND = 512


HIGH = lax.Precision.HIGHEST
EPS = 1e-06


def extended(cells, sides, width):
    for axis, dim in sides:
        count = lax.axis_size(axis)
        head = lax.slice_in_dim(cells, 0, width, axis=dim)
        tail = lax.slice_in_dim(cells, cells.shape[dim] - width, cells.shape[dim], axis=dim)
        cells = jnp.concatenate(
            [
                lax.ppermute(tail, axis, [(i, (i + 1) % count) for i in range(count)]),
                cells,
                lax.ppermute(head, axis, [((i + 1) % count, i) for i in range(count)]),
            ],
            axis=dim,
        )
    return cells


def from_behind(value, axis, steps):
    count = lax.axis_size(axis)
    pairs = [(source, (source + steps) % count) for source in range(count)]
    return lax.ppermute(value, axis, pairs)


def silu_slope(value):
    sigma = jax.nn.sigmoid(value)
    return sigma * (1.0 + value * (1.0 - sigma))


def block_offsets(count, reach_blocks):
    chosen = []
    taken = []
    for distance in range(reach_blocks + 1):
        for offset in (distance, -distance):
            if offset % count not in taken:
                taken.append(offset % count)
                chosen.append(offset)
    return chosen


def split_heads(array, heads):
    return array.reshape(array.shape[0], array.shape[1], heads, array.shape[2] // heads)


def band_scores(query, keys, prior, query_places, key_places, limit, cycle_tokens, factor):
    scores = jnp.einsum("sqhe,skhe->shqk", query, keys, preferred_element_type=jnp.float32) * factor
    scores = scores + prior.astype(jnp.float32)[:, None, None, :]
    apart = (key_places[None, :] - query_places[:, None]) % cycle_tokens
    apart = jnp.minimum(apart, cycle_tokens - apart)
    inside = apart[None, None] <= limit[:, None, None, None]
    return (scores, inside)


def per_device(
    genotypes,
    key_prior,
    band_reach,
    cotangent,
    conv_weight,
    conv_bias,
    mix_weight,
    embed_weight,
    norm_gain,
    attn_weight,
):
    sims, haps, sites = genotypes.shape
    patch = conv_weight.shape[0]
    local = sites // patch
    width = attn_weight.shape[1]
    heads = HEADS
    factor = HEAD_DIM ** (-0.5)
    count = lax.axis_size("sites")
    cycle_tokens = local * count
    place = lax.axis_index("sites")
    ordinal = jnp.arange(local, dtype=jnp.int32)
    patches = genotypes.astype(jnp.float32).reshape(sims, haps, local, patch)
    pre = (
        jnp.einsum("shtk,kc->shct", patches, conv_weight, precision=HIGH)
        + conv_bias[None, None, :, None]
    )
    pooled = jnp.mean(jax.nn.silu(pre), axis=1)
    pooled_wide = extended(pooled, (("sites", 2),), 1)
    mixed = jnp.zeros((sims, mix_weight.shape[2], local), jnp.float32)
    for shift_by in (-1, 0, 1):
        mixed = mixed + jnp.einsum(
            "co,sct->sot",
            mix_weight[shift_by + 1],
            pooled_wide[:, :, 1 + shift_by : 1 + shift_by + local],
            precision=HIGH,
        )
    activated = jax.nn.silu(mixed)
    embedded = jnp.einsum("sct,cd->std", activated, embed_weight, precision=HIGH).astype(
        jnp.bfloat16
    )
    wide = embedded.astype(jnp.float32)
    inverse = lax.rsqrt(jnp.mean(wide * wide, axis=2, keepdims=True) + EPS)
    normed = (wide * inverse * norm_gain).astype(jnp.bfloat16)
    query = jnp.einsum(
        "std,de->ste", normed, attn_weight[0], preferred_element_type=jnp.float32
    ).astype(jnp.bfloat16)
    keys = jnp.einsum(
        "std,de->ste", normed, attn_weight[1], preferred_element_type=jnp.float32
    ).astype(jnp.bfloat16)
    values = jnp.einsum(
        "std,de->ste", normed, attn_weight[2], preferred_element_type=jnp.float32
    ).astype(jnp.bfloat16)
    query_heads = split_heads(query, heads)
    key_heads = split_heads(keys, heads)
    value_heads = split_heads(values, heads)
    reach_blocks = -(-BAND // local)
    offsets = block_offsets(count, reach_blocks)
    packed = jnp.concatenate(
        [keys, values, key_prior[:, :, None]], axis=2
    )
    gathered = {0: packed}
    for offset in offsets[1:]:
        gathered[offset] = from_behind(packed, "sites", -offset)
    packed_cat = jnp.concatenate([gathered[offset] for offset in offsets], axis=1)
    key_cat = split_heads(packed_cat[:, :, :width], heads)
    value_cat = split_heads(packed_cat[:, :, width : 2 * width], heads)
    prior_cat = packed_cat[:, :, 2 * width]
    key_places = jnp.concatenate([(place + offset) % count * local + ordinal for offset in offsets])
    query_places = place * local + ordinal
    scores, inside = band_scores(
        query_heads, key_cat, prior_cat, query_places, key_places, band_reach, cycle_tokens, factor
    )
    row_top = jnp.max(jnp.where(inside, scores, -jnp.inf), axis=-1, keepdims=True)
    lifted = jnp.where(inside, jnp.exp(scores - row_top), 0.0)
    row_total = jnp.sum(lifted, axis=-1, keepdims=True)
    prob = lifted / row_total
    prob_half = prob.astype(jnp.bfloat16)
    attended_full = jnp.einsum(
        "shqk,skhe->sqhe", prob_half, value_cat, preferred_element_type=jnp.float32
    )
    attended = attended_full.astype(jnp.bfloat16).reshape(sims, local, width)
    grad_attended = jnp.einsum(
        "std,ed->ste", cotangent, attn_weight[3], preferred_element_type=jnp.float32
    ).astype(jnp.bfloat16)
    grad_heads = split_heads(grad_attended, heads)
    delta = jnp.einsum("sqhe,sqhe->shq", grad_heads.astype(jnp.float32), attended_full)
    grad_prob = jnp.einsum(
        "sqhe,skhe->shqk", grad_heads, value_cat, preferred_element_type=jnp.float32
    )
    grad_scores = (prob * (grad_prob - delta[..., None]) * factor).astype(jnp.bfloat16)
    grad_query = jnp.einsum(
        "shqk,skhe->sqhe", grad_scores, key_cat, preferred_element_type=jnp.float32
    ).astype(jnp.bfloat16)
    grad_query = grad_query.reshape(sims, local, width)
    key_part = jnp.einsum(
        "shqk,sqhe->skhe", grad_scores, query_heads, preferred_element_type=jnp.float32
    )
    value_part = jnp.einsum(
        "shqk,sqhe->skhe", prob_half, grad_heads, preferred_element_type=jnp.float32
    )
    key_sum = key_part[:, 0:local]
    value_sum = value_part[:, 0:local]
    for position, offset in enumerate(offsets[1:], start=1):
        lower = position * local
        both = jnp.concatenate(
            [key_part[:, lower : lower + local], value_part[:, lower : lower + local]], axis=2
        ).astype(jnp.bfloat16)
        back = from_behind(both, "sites", offset).astype(jnp.float32)
        key_sum = key_sum + back[:, :, :heads]
        value_sum = value_sum + back[:, :, heads:]
    grad_keys = key_sum.astype(jnp.bfloat16).reshape(sims, local, width)
    grad_values = value_sum.astype(jnp.bfloat16).reshape(sims, local, width)
    term_query = jnp.einsum("std,ste->de", normed, grad_query, preferred_element_type=jnp.float32)
    term_keys = jnp.einsum("std,ste->de", normed, grad_keys, preferred_element_type=jnp.float32)
    term_values = jnp.einsum("std,ste->de", normed, grad_values, preferred_element_type=jnp.float32)
    term_output = jnp.einsum("std,ste->de", attended, cotangent, preferred_element_type=jnp.float32)
    flat_terms = jnp.stack([term_query, term_keys, term_values, term_output]).reshape(-1)
    grad_attention = lax.psum_scatter(
        lax.psum_scatter(flat_terms, "sims", scatter_dimension=0, tiled=True),
        "sites",
        scatter_dimension=0,
        tiled=True,
    )
    grad_normed = jnp.einsum(
        "ste,de->std", grad_query, attn_weight[0], preferred_element_type=jnp.float32
    )
    grad_normed = grad_normed + jnp.einsum(
        "ste,de->std", grad_keys, attn_weight[1], preferred_element_type=jnp.float32
    )
    grad_normed = grad_normed + jnp.einsum(
        "ste,de->std", grad_values, attn_weight[2], preferred_element_type=jnp.float32
    )
    term_gain = jnp.sum(grad_normed * wide * inverse, axis=(0, 1))
    scaled = grad_normed * norm_gain
    grad_embedded = (
        inverse * scaled - wide * inverse**3 * jnp.sum(scaled * wide, axis=2, keepdims=True) / width
    )
    grad_embedded = grad_embedded + cotangent.astype(jnp.float32)
    term_embed = jnp.einsum("sct,std->cd", activated, grad_embedded, precision=HIGH)
    grad_mixed = jnp.einsum(
        "std,od->sot", grad_embedded, embed_weight, precision=HIGH
    ) * silu_slope(mixed)
    mixed_wide = extended(grad_mixed.astype(jnp.bfloat16), (("sites", 2),), 1).astype(
        grad_mixed.dtype
    )
    mix_terms = []
    grad_pooled = jnp.zeros(pooled.shape, jnp.float32)
    for shift_by in (-1, 0, 1):
        mix_terms.append(
            jnp.einsum(
                "sct,sot->co",
                pooled_wide[:, :, 1 + shift_by : 1 + shift_by + local],
                grad_mixed,
                precision=HIGH,
            )
        )
        grad_pooled = grad_pooled + jnp.einsum(
            "co,sot->sct",
            mix_weight[shift_by + 1],
            mixed_wide[:, :, 1 - shift_by : 1 - shift_by + local],
            precision=HIGH,
        )
    grad_pre = (grad_pooled / haps)[:, None] * silu_slope(pre)
    term_conv = jnp.einsum("shtk,shct->kc", patches, grad_pre, precision=HIGH)
    term_bias = jnp.sum(grad_pre, axis=(0, 1, 3))
    small = (term_conv, term_bias, jnp.stack(mix_terms), term_embed, term_gain)
    flat_small = lax.psum(jnp.concatenate([t.reshape(-1) for t in small]), ("sims", "sites"))
    pieces = []
    lower = 0
    for t in small:
        pieces.append(flat_small[lower : lower + t.size].reshape(t.shape))
        lower += t.size
    grad_conv, grad_bias, grad_mix, grad_embed, grad_gain = pieces
    return (grad_attention, grad_conv, grad_bias, grad_mix, grad_embed, grad_gain)


def solution(mesh):
    placed = (
        P("sims", None, "sites"),
        P("sims", "sites"),
        P("sims"),
        P("sims", "sites", None),
        P(),
        P(),
        P(),
        P(),
        P(),
        P(),
    )
    return jax.shard_map(
        per_device,
        mesh=mesh,
        in_specs=placed,
        out_specs=(P(("sims", "sites")), P(), P(), P(), P(), P()),
        check_vma=False,
    )
```

```python
import jax
import jax.numpy as jnp
from jax import lax
from jax.sharding import PartitionSpec as P

HEADS = 8
HEAD_DIM = 64
BAND = 512


HIGH = lax.Precision.HIGHEST
EPS = 1e-06


def extended(cells, sides, width):
    for axis, dim in sides:
        count = lax.axis_size(axis)
        head = lax.slice_in_dim(cells, 0, width, axis=dim)
        tail = lax.slice_in_dim(cells, cells.shape[dim] - width, cells.shape[dim], axis=dim)
        cells = jnp.concatenate(
            [
                lax.ppermute(tail, axis, [(i, (i + 1) % count) for i in range(count)]),
                cells,
                lax.ppermute(head, axis, [((i + 1) % count, i) for i in range(count)]),
            ],
            axis=dim,
        )
    return cells


def from_behind(value, axis, steps):
    count = lax.axis_size(axis)
    pairs = [(source, (source + steps) % count) for source in range(count)]
    return lax.ppermute(value, axis, pairs)


def silu_slope(value):
    sigma = jax.nn.sigmoid(value)
    return sigma * (1.0 + value * (1.0 - sigma))


def block_offsets(count, reach_blocks):
    chosen = []
    taken = []
    for distance in range(reach_blocks + 1):
        for offset in (distance, -distance):
            if offset % count not in taken:
                taken.append(offset % count)
                chosen.append(offset)
    return chosen


def split_heads(array, heads):
    return array.reshape(array.shape[0], array.shape[1], heads, array.shape[2] // heads)


def band_scores(query, keys, prior, query_places, key_places, limit, cycle_tokens, factor):
    scores = jnp.einsum("sqhe,skhe->shqk", query, keys, preferred_element_type=jnp.float32) * factor
    scores = scores + prior.astype(jnp.float32)[:, None, None, :]
    apart = (key_places[None, :] - query_places[:, None]) % cycle_tokens
    apart = jnp.minimum(apart, cycle_tokens - apart)
    inside = apart[None, None] <= limit[:, None, None, None]
    return (scores, inside)


def bit_count(size):
    bits = size.bit_length() - 1
    assert 1 << bits == size
    return bits


def butterfly_sum(flat, small):
    sims_bits = bit_count(lax.axis_size("sims"))
    sites_bits = bit_count(lax.axis_size("sites"))
    total_bits = sims_bits + sites_bits
    chunk = flat.shape[0] >> total_bits
    cells = flat.reshape((2,) * total_bits + (chunk,))
    dim_of = {}
    for bit in range(sims_bits):
        dim_of[("sims", bit)] = sims_bits - 1 - bit
    for bit in range(sites_bits):
        dim_of[("sites", bit)] = total_bits - 1 - bit
    order = [("sims", 0), ("sims", sims_bits - 1)]
    pending = [("sims", b) for b in range(1, sims_bits - 1)]
    pending_sites = [("sites", b) for b in (2, 3, 0, 1) if b < sites_bits]
    pending_sites += [("sites", b) for b in range(sites_bits) if ("sites", b) not in pending_sites]
    while pending or pending_sites:
        if pending:
            order.append(pending.pop(0))
        if pending_sites:
            order.append(pending_sites.pop(0))
    order = list(dict.fromkeys(order))
    kept_dims = list(range(total_bits))
    for axis, bit in order:
        dim = kept_dims.index(dim_of[(axis, bit)])
        kept_dims.pop(dim)
        count = lax.axis_size(axis)
        mine = (lax.axis_index(axis) >> bit) & 1
        keep = lax.dynamic_index_in_dim(cells, mine, axis=dim, keepdims=False)
        send = lax.dynamic_index_in_dim(cells, 1 - mine, axis=dim, keepdims=False)
        shape = keep.shape
        outgoing = jnp.concatenate([send.reshape(-1), small])
        pairs = [(i, i ^ (1 << bit)) for i in range(count)]
        incoming = lax.ppermute(outgoing, axis, pairs)
        cells = keep + incoming[: keep.size].reshape(shape)
        small = small + incoming[keep.size :]
    return cells.reshape(chunk), small


def per_device(
    genotypes,
    key_prior,
    band_reach,
    cotangent,
    conv_weight,
    conv_bias,
    mix_weight,
    embed_weight,
    norm_gain,
    attn_weight,
):
    sims, haps, sites = genotypes.shape
    patch = conv_weight.shape[0]
    local = sites // patch
    width = attn_weight.shape[1]
    heads = HEADS
    factor = HEAD_DIM ** (-0.5)
    count = lax.axis_size("sites")
    cycle_tokens = local * count
    place = lax.axis_index("sites")
    ordinal = jnp.arange(local, dtype=jnp.int32)
    patches = genotypes.astype(jnp.float32).reshape(sims, haps, local, patch)
    pre = (
        jnp.einsum("shtk,kc->shct", patches, conv_weight, precision=HIGH)
        + conv_bias[None, None, :, None]
    )
    pooled = jnp.mean(jax.nn.silu(pre), axis=1)
    pooled_wide = extended(pooled, (("sites", 2),), 1)
    mixed = jnp.zeros((sims, mix_weight.shape[2], local), jnp.float32)
    for shift_by in (-1, 0, 1):
        mixed = mixed + jnp.einsum(
            "co,sct->sot",
            mix_weight[shift_by + 1],
            pooled_wide[:, :, 1 + shift_by : 1 + shift_by + local],
            precision=HIGH,
        )
    activated = jax.nn.silu(mixed)
    embedded = jnp.einsum("sct,cd->std", activated, embed_weight, precision=HIGH).astype(
        jnp.bfloat16
    )
    wide = embedded.astype(jnp.float32)
    inverse = lax.rsqrt(jnp.mean(wide * wide, axis=2, keepdims=True) + EPS)
    normed = (wide * inverse * norm_gain).astype(jnp.bfloat16)
    query = jnp.einsum(
        "std,de->ste", normed, attn_weight[0], preferred_element_type=jnp.float32
    ).astype(jnp.bfloat16)
    keys = jnp.einsum(
        "std,de->ste", normed, attn_weight[1], preferred_element_type=jnp.float32
    ).astype(jnp.bfloat16)
    values = jnp.einsum(
        "std,de->ste", normed, attn_weight[2], preferred_element_type=jnp.float32
    ).astype(jnp.bfloat16)
    query_heads = split_heads(query, heads)
    key_heads = split_heads(keys, heads)
    value_heads = split_heads(values, heads)
    reach_blocks = -(-BAND // local)
    offsets = block_offsets(count, reach_blocks)
    packed = jnp.concatenate(
        [keys, values, key_prior[:, :, None]], axis=2
    )
    gathered = {0: packed}
    for offset in offsets[1:]:
        gathered[offset] = from_behind(packed, "sites", -offset)
    packed_cat = jnp.concatenate([gathered[offset] for offset in offsets], axis=1)
    key_cat = split_heads(packed_cat[:, :, :width], heads)
    value_cat = split_heads(packed_cat[:, :, width : 2 * width], heads)
    prior_cat = packed_cat[:, :, 2 * width]
    key_places = jnp.concatenate([(place + offset) % count * local + ordinal for offset in offsets])
    query_places = place * local + ordinal
    scores, inside = band_scores(
        query_heads, key_cat, prior_cat, query_places, key_places, band_reach, cycle_tokens, factor
    )
    row_top = jnp.max(jnp.where(inside, scores, -jnp.inf), axis=-1, keepdims=True)
    lifted = jnp.where(inside, jnp.exp(scores - row_top), 0.0)
    row_total = jnp.sum(lifted, axis=-1, keepdims=True)
    prob = lifted / row_total
    prob_half = prob.astype(jnp.bfloat16)
    attended_full = jnp.einsum(
        "shqk,skhe->sqhe", prob_half, value_cat, preferred_element_type=jnp.float32
    )
    attended = attended_full.astype(jnp.bfloat16).reshape(sims, local, width)
    grad_attended = jnp.einsum(
        "std,ed->ste", cotangent, attn_weight[3], preferred_element_type=jnp.float32
    ).astype(jnp.bfloat16)
    grad_heads = split_heads(grad_attended, heads)
    delta = jnp.einsum("sqhe,sqhe->shq", grad_heads.astype(jnp.float32), attended_full)
    grad_prob = jnp.einsum(
        "sqhe,skhe->shqk", grad_heads, value_cat, preferred_element_type=jnp.float32
    )
    grad_scores = (prob * (grad_prob - delta[..., None]) * factor).astype(jnp.bfloat16)
    grad_query = jnp.einsum(
        "shqk,skhe->sqhe", grad_scores, key_cat, preferred_element_type=jnp.float32
    ).astype(jnp.bfloat16)
    grad_query = grad_query.reshape(sims, local, width)
    key_part = jnp.einsum(
        "shqk,sqhe->skhe", grad_scores, query_heads, preferred_element_type=jnp.float32
    )
    value_part = jnp.einsum(
        "shqk,sqhe->skhe", prob_half, grad_heads, preferred_element_type=jnp.float32
    )
    key_sum = key_part[:, 0:local]
    value_sum = value_part[:, 0:local]
    for position, offset in enumerate(offsets[1:], start=1):
        lower = position * local
        both = jnp.concatenate(
            [key_part[:, lower : lower + local], value_part[:, lower : lower + local]], axis=2
        ).astype(jnp.bfloat16)
        back = from_behind(both, "sites", offset).astype(jnp.float32)
        key_sum = key_sum + back[:, :, :heads]
        value_sum = value_sum + back[:, :, heads:]
    grad_keys = key_sum.astype(jnp.bfloat16).reshape(sims, local, width)
    grad_values = value_sum.astype(jnp.bfloat16).reshape(sims, local, width)
    term_query = jnp.einsum("std,ste->de", normed, grad_query, preferred_element_type=jnp.float32)
    term_keys = jnp.einsum("std,ste->de", normed, grad_keys, preferred_element_type=jnp.float32)
    term_values = jnp.einsum("std,ste->de", normed, grad_values, preferred_element_type=jnp.float32)
    term_output = jnp.einsum("std,ste->de", attended, cotangent, preferred_element_type=jnp.float32)
    flat_terms = jnp.stack([term_query, term_keys, term_values, term_output]).reshape(-1)
    grad_normed = jnp.einsum(
        "ste,de->std", grad_query, attn_weight[0], preferred_element_type=jnp.float32
    )
    grad_normed = grad_normed + jnp.einsum(
        "ste,de->std", grad_keys, attn_weight[1], preferred_element_type=jnp.float32
    )
    grad_normed = grad_normed + jnp.einsum(
        "ste,de->std", grad_values, attn_weight[2], preferred_element_type=jnp.float32
    )
    term_gain = jnp.sum(grad_normed * wide * inverse, axis=(0, 1))
    scaled = grad_normed * norm_gain
    grad_embedded = (
        inverse * scaled - wide * inverse**3 * jnp.sum(scaled * wide, axis=2, keepdims=True) / width
    )
    grad_embedded = grad_embedded + cotangent.astype(jnp.float32)
    term_embed = jnp.einsum("sct,std->cd", activated, grad_embedded, precision=HIGH)
    grad_mixed = jnp.einsum(
        "std,od->sot", grad_embedded, embed_weight, precision=HIGH
    ) * silu_slope(mixed)
    mixed_wide = extended(grad_mixed.astype(jnp.bfloat16), (("sites", 2),), 1).astype(
        grad_mixed.dtype
    )
    mix_terms = []
    grad_pooled = jnp.zeros(pooled.shape, jnp.float32)
    for shift_by in (-1, 0, 1):
        mix_terms.append(
            jnp.einsum(
                "sct,sot->co",
                pooled_wide[:, :, 1 + shift_by : 1 + shift_by + local],
                grad_mixed,
                precision=HIGH,
            )
        )
        grad_pooled = grad_pooled + jnp.einsum(
            "co,sot->sct",
            mix_weight[shift_by + 1],
            mixed_wide[:, :, 1 - shift_by : 1 - shift_by + local],
            precision=HIGH,
        )
    grad_pre = (grad_pooled / haps)[:, None] * silu_slope(pre)
    term_conv = jnp.einsum("shtk,shct->kc", patches, grad_pre, precision=HIGH)
    term_bias = jnp.sum(grad_pre, axis=(0, 1, 3))
    small = (term_conv, term_bias, jnp.stack(mix_terms), term_embed, term_gain)
    flat_small = jnp.concatenate([t.reshape(-1) for t in small])
    grad_attention, flat_small = butterfly_sum(flat_terms, flat_small)
    pieces = []
    lower = 0
    for t in small:
        pieces.append(flat_small[lower : lower + t.size].reshape(t.shape))
        lower += t.size
    grad_conv, grad_bias, grad_mix, grad_embed, grad_gain = pieces
    return (grad_attention, grad_conv, grad_bias, grad_mix, grad_embed, grad_gain)


def solution(mesh):
    placed = (
        P("sims", None, "sites"),
        P("sims", "sites"),
        P("sims"),
        P("sims", "sites", None),
        P(),
        P(),
        P(),
        P(),
        P(),
        P(),
    )
    return jax.shard_map(
        per_device,
        mesh=mesh,
        in_specs=placed,
        out_specs=(P(("sims", "sites")), P(), P(), P(), P(), P()),
        check_vma=False,
    )
```

```python
import jax
import jax.numpy as jnp
from jax import lax
from jax.sharding import PartitionSpec as P

HEADS = 8
HEAD_DIM = 64
BAND = 512


HIGH = lax.Precision.HIGHEST
EPS = 1e-06


def extended(cells, sides, width):
    for axis, dim in sides:
        count = lax.axis_size(axis)
        head = lax.slice_in_dim(cells, 0, width, axis=dim)
        tail = lax.slice_in_dim(cells, cells.shape[dim] - width, cells.shape[dim], axis=dim)
        cells = jnp.concatenate(
            [
                lax.ppermute(tail, axis, [(i, (i + 1) % count) for i in range(count)]),
                cells,
                lax.ppermute(head, axis, [((i + 1) % count, i) for i in range(count)]),
            ],
            axis=dim,
        )
    return cells


def from_behind(value, axis, steps):
    count = lax.axis_size(axis)
    pairs = [(source, (source + steps) % count) for source in range(count)]
    return lax.ppermute(value, axis, pairs)


def silu_slope(value):
    sigma = jax.nn.sigmoid(value)
    return sigma * (1.0 + value * (1.0 - sigma))


def block_offsets(count, reach_blocks):
    chosen = []
    taken = []
    for distance in range(reach_blocks + 1):
        for offset in (distance, -distance):
            if offset % count not in taken:
                taken.append(offset % count)
                chosen.append(offset)
    return chosen


def split_heads(array, heads):
    return array.reshape(array.shape[0], array.shape[1], heads, array.shape[2] // heads)


def band_scores(query, keys, prior, query_places, key_places, limit, cycle_tokens, factor):
    scores = jnp.einsum("sqhe,skhe->shqk", query, keys, preferred_element_type=jnp.float32) * factor
    scores = scores + prior.astype(jnp.float32)[:, None, None, :]
    apart = (key_places[None, :] - query_places[:, None]) % cycle_tokens
    apart = jnp.minimum(apart, cycle_tokens - apart)
    inside = apart[None, None] <= limit[:, None, None, None]
    return (scores, inside)


def bit_count(size):
    bits = size.bit_length() - 1
    assert 1 << bits == size
    return bits


def butterfly_sum(flat, small):
    sims_bits = bit_count(lax.axis_size("sims"))
    sites_bits = bit_count(lax.axis_size("sites"))
    total_bits = sims_bits + sites_bits
    chunk = flat.shape[0] >> total_bits
    dim_of = {}
    for bit in range(sims_bits):
        dim_of[("sims", bit)] = sims_bits - 1 - bit
    for bit in range(sites_bits):
        dim_of[("sites", bit)] = total_bits - 1 - bit
    order = [("sims", 0), ("sims", sims_bits - 1)]
    pending = [("sims", b) for b in range(1, sims_bits - 1)]
    pending_sites = [("sites", b) for b in (2, 3, 0, 1) if b < sites_bits]
    pending_sites += [("sites", b) for b in range(sites_bits) if ("sites", b) not in pending_sites]
    while pending or pending_sites:
        if pending:
            order.append(pending.pop(0))
        if pending_sites:
            order.append(pending_sites.pop(0))
    order = list(dict.fromkeys(order))
    cells = flat.reshape((2,) * total_bits + (chunk // 512, 512))
    cells = cells.transpose([dim_of[o] for o in order] + [total_bits, total_bits + 1])
    current = cells.reshape(-1)
    for axis, bit in order:
        count = lax.axis_size(axis)
        half = current.shape[0] // 2
        mine = (lax.axis_index(axis) >> bit) & 1
        keep = lax.dynamic_slice_in_dim(current, mine * half, half)
        send = lax.dynamic_slice_in_dim(current, (1 - mine) * half, half)
        outgoing = jnp.concatenate([send, small])
        pairs = [(i, i ^ (1 << bit)) for i in range(count)]
        incoming = lax.ppermute(outgoing, axis, pairs)
        current = keep + incoming[:half]
        small = small + incoming[half:]
    return current, small

def per_device(
    genotypes,
    key_prior,
    band_reach,
    cotangent,
    conv_weight,
    conv_bias,
    mix_weight,
    embed_weight,
    norm_gain,
    attn_weight,
):
    sims, haps, sites = genotypes.shape
    patch = conv_weight.shape[0]
    local = sites // patch
    width = attn_weight.shape[1]
    heads = HEADS
    factor = HEAD_DIM ** (-0.5)
    count = lax.axis_size("sites")
    cycle_tokens = local * count
    place = lax.axis_index("sites")
    ordinal = jnp.arange(local, dtype=jnp.int32)
    patches = genotypes.astype(jnp.float32).reshape(sims, haps, local, patch)
    pre = (
        jnp.einsum("shtk,kc->shct", patches, conv_weight, precision=HIGH)
        + conv_bias[None, None, :, None]
    )
    pooled = jnp.mean(jax.nn.silu(pre), axis=1)
    pooled_wide = extended(pooled, (("sites", 2),), 1)
    mixed = jnp.zeros((sims, mix_weight.shape[2], local), jnp.float32)
    for shift_by in (-1, 0, 1):
        mixed = mixed + jnp.einsum(
            "co,sct->sot",
            mix_weight[shift_by + 1],
            pooled_wide[:, :, 1 + shift_by : 1 + shift_by + local],
            precision=HIGH,
        )
    activated = jax.nn.silu(mixed)
    embedded = jnp.einsum("sct,cd->std", activated, embed_weight, precision=HIGH).astype(
        jnp.bfloat16
    )
    wide = embedded.astype(jnp.float32)
    inverse = lax.rsqrt(jnp.mean(wide * wide, axis=2, keepdims=True) + EPS)
    normed = (wide * inverse * norm_gain).astype(jnp.bfloat16)
    query = jnp.einsum(
        "std,de->ste", normed, attn_weight[0], preferred_element_type=jnp.float32
    ).astype(jnp.bfloat16)
    keys = jnp.einsum(
        "std,de->ste", normed, attn_weight[1], preferred_element_type=jnp.float32
    ).astype(jnp.bfloat16)
    values = jnp.einsum(
        "std,de->ste", normed, attn_weight[2], preferred_element_type=jnp.float32
    ).astype(jnp.bfloat16)
    query_heads = split_heads(query, heads)
    key_heads = split_heads(keys, heads)
    value_heads = split_heads(values, heads)
    reach_blocks = -(-BAND // local)
    offsets = block_offsets(count, reach_blocks)
    packed = jnp.concatenate(
        [keys, values, key_prior[:, :, None]], axis=2
    )
    gathered = {0: packed}
    for offset in offsets[1:]:
        gathered[offset] = from_behind(packed, "sites", -offset)
    packed_cat = jnp.concatenate([gathered[offset] for offset in offsets], axis=1)
    key_cat = split_heads(packed_cat[:, :, :width], heads)
    value_cat = split_heads(packed_cat[:, :, width : 2 * width], heads)
    prior_cat = packed_cat[:, :, 2 * width]
    key_places = jnp.concatenate([(place + offset) % count * local + ordinal for offset in offsets])
    query_places = place * local + ordinal
    scores, inside = band_scores(
        query_heads, key_cat, prior_cat, query_places, key_places, band_reach, cycle_tokens, factor
    )
    row_top = jnp.max(jnp.where(inside, scores, -jnp.inf), axis=-1, keepdims=True)
    lifted = jnp.where(inside, jnp.exp(scores - row_top), 0.0)
    row_total = jnp.sum(lifted, axis=-1, keepdims=True)
    prob = lifted / row_total
    prob_half = prob.astype(jnp.bfloat16)
    attended_full = jnp.einsum(
        "shqk,skhe->sqhe", prob_half, value_cat, preferred_element_type=jnp.float32
    )
    attended = attended_full.astype(jnp.bfloat16).reshape(sims, local, width)
    grad_attended = jnp.einsum(
        "std,ed->ste", cotangent, attn_weight[3], preferred_element_type=jnp.float32
    ).astype(jnp.bfloat16)
    grad_heads = split_heads(grad_attended, heads)
    delta = jnp.einsum("sqhe,sqhe->shq", grad_heads.astype(jnp.float32), attended_full)
    grad_prob = jnp.einsum(
        "sqhe,skhe->shqk", grad_heads, value_cat, preferred_element_type=jnp.float32
    )
    grad_scores = (prob * (grad_prob - delta[..., None]) * factor).astype(jnp.bfloat16)
    grad_query = jnp.einsum(
        "shqk,skhe->sqhe", grad_scores, key_cat, preferred_element_type=jnp.float32
    ).astype(jnp.bfloat16)
    grad_query = grad_query.reshape(sims, local, width)
    key_part = jnp.einsum(
        "shqk,sqhe->skhe", grad_scores, query_heads, preferred_element_type=jnp.float32
    )
    value_part = jnp.einsum(
        "shqk,sqhe->skhe", prob_half, grad_heads, preferred_element_type=jnp.float32
    )
    key_sum = key_part[:, 0:local]
    value_sum = value_part[:, 0:local]
    for position, offset in enumerate(offsets[1:], start=1):
        lower = position * local
        both = jnp.concatenate(
            [key_part[:, lower : lower + local], value_part[:, lower : lower + local]], axis=2
        ).astype(jnp.bfloat16)
        back = from_behind(both, "sites", offset).astype(jnp.float32)
        key_sum = key_sum + back[:, :, :heads]
        value_sum = value_sum + back[:, :, heads:]
    grad_keys = key_sum.astype(jnp.bfloat16).reshape(sims, local, width)
    grad_values = value_sum.astype(jnp.bfloat16).reshape(sims, local, width)
    term_query = jnp.einsum("std,ste->de", normed, grad_query, preferred_element_type=jnp.float32)
    term_keys = jnp.einsum("std,ste->de", normed, grad_keys, preferred_element_type=jnp.float32)
    term_values = jnp.einsum("std,ste->de", normed, grad_values, preferred_element_type=jnp.float32)
    term_output = jnp.einsum("std,ste->de", attended, cotangent, preferred_element_type=jnp.float32)
    flat_terms = jnp.stack([term_query, term_keys, term_values, term_output]).reshape(-1)
    grad_normed = jnp.einsum(
        "ste,de->std", grad_query, attn_weight[0], preferred_element_type=jnp.float32
    )
    grad_normed = grad_normed + jnp.einsum(
        "ste,de->std", grad_keys, attn_weight[1], preferred_element_type=jnp.float32
    )
    grad_normed = grad_normed + jnp.einsum(
        "ste,de->std", grad_values, attn_weight[2], preferred_element_type=jnp.float32
    )
    term_gain = jnp.sum(grad_normed * wide * inverse, axis=(0, 1))
    scaled = grad_normed * norm_gain
    grad_embedded = (
        inverse * scaled - wide * inverse**3 * jnp.sum(scaled * wide, axis=2, keepdims=True) / width
    )
    grad_embedded = grad_embedded + cotangent.astype(jnp.float32)
    term_embed = jnp.einsum("sct,std->cd", activated, grad_embedded, precision=HIGH)
    grad_mixed = jnp.einsum(
        "std,od->sot", grad_embedded, embed_weight, precision=HIGH
    ) * silu_slope(mixed)
    mixed_wide = extended(grad_mixed.astype(jnp.bfloat16), (("sites", 2),), 1).astype(
        grad_mixed.dtype
    )
    mix_terms = []
    grad_pooled = jnp.zeros(pooled.shape, jnp.float32)
    for shift_by in (-1, 0, 1):
        mix_terms.append(
            jnp.einsum(
                "sct,sot->co",
                pooled_wide[:, :, 1 + shift_by : 1 + shift_by + local],
                grad_mixed,
                precision=HIGH,
            )
        )
        grad_pooled = grad_pooled + jnp.einsum(
            "co,sot->sct",
            mix_weight[shift_by + 1],
            mixed_wide[:, :, 1 - shift_by : 1 - shift_by + local],
            precision=HIGH,
        )
    grad_pre = (grad_pooled / haps)[:, None] * silu_slope(pre)
    term_conv = jnp.einsum("shtk,shct->kc", patches, grad_pre, precision=HIGH)
    term_bias = jnp.sum(grad_pre, axis=(0, 1, 3))
    small = (term_conv, term_bias, jnp.stack(mix_terms), term_embed, term_gain)
    flat_small = jnp.concatenate([t.reshape(-1) for t in small])
    grad_attention, flat_small = butterfly_sum(flat_terms, flat_small)
    pieces = []
    lower = 0
    for t in small:
        pieces.append(flat_small[lower : lower + t.size].reshape(t.shape))
        lower += t.size
    grad_conv, grad_bias, grad_mix, grad_embed, grad_gain = pieces
    return (grad_attention, grad_conv, grad_bias, grad_mix, grad_embed, grad_gain)


def solution(mesh):
    placed = (
        P("sims", None, "sites"),
        P("sims", "sites"),
        P("sims"),
        P("sims", "sites", None),
        P(),
        P(),
        P(),
        P(),
        P(),
        P(),
    )
    return jax.shard_map(
        per_device,
        mesh=mesh,
        in_specs=placed,
        out_specs=(P(("sims", "sites")), P(), P(), P(), P(), P()),
        check_vma=False,
    )
```

```python
import functools

import jax
import jax.numpy as jnp
from jax import lax
from jax.experimental import pallas as pl
from jax.experimental.pallas import tpu as pltpu
from jax.sharding import PartitionSpec as P

HEADS = 8
HEAD_DIM = 64
BAND = 512


HIGH = lax.Precision.HIGHEST
EPS = 1e-06


def extended(cells, sides, width):
    for axis, dim in sides:
        count = lax.axis_size(axis)
        head = lax.slice_in_dim(cells, 0, width, axis=dim)
        tail = lax.slice_in_dim(cells, cells.shape[dim] - width, cells.shape[dim], axis=dim)
        cells = jnp.concatenate(
            [
                lax.ppermute(tail, axis, [(i, (i + 1) % count) for i in range(count)]),
                cells,
                lax.ppermute(head, axis, [((i + 1) % count, i) for i in range(count)]),
            ],
            axis=dim,
        )
    return cells


def from_behind(value, axis, steps):
    count = lax.axis_size(axis)
    pairs = [(source, (source + steps) % count) for source in range(count)]
    return lax.ppermute(value, axis, pairs)


def silu_slope(value):
    sigma = jax.nn.sigmoid(value)
    return sigma * (1.0 + value * (1.0 - sigma))


def block_offsets(count, reach_blocks):
    chosen = []
    taken = []
    for distance in range(reach_blocks + 1):
        for offset in (distance, -distance):
            if offset % count not in taken:
                taken.append(offset % count)
                chosen.append(offset)
    return chosen


def split_heads(array, heads):
    return array.reshape(array.shape[0], array.shape[1], heads, array.shape[2] // heads)


def band_scores(query, keys, prior, query_places, key_places, limit, cycle_tokens, factor):
    scores = jnp.einsum("sqhe,skhe->shqk", query, keys, preferred_element_type=jnp.float32) * factor
    scores = scores + prior.astype(jnp.float32)[:, None, None, :]
    apart = (key_places[None, :] - query_places[:, None]) % cycle_tokens
    apart = jnp.minimum(apart, cycle_tokens - apart)
    inside = apart[None, None] <= limit[:, None, None, None]
    return (scores, inside)


def bit_count(size):
    bits = size.bit_length() - 1
    assert 1 << bits == size
    return bits


def butterfly_sum(flat, small):
    sims_bits = bit_count(lax.axis_size("sims"))
    sites_bits = bit_count(lax.axis_size("sites"))
    total_bits = sims_bits + sites_bits
    chunk = flat.shape[0] >> total_bits
    dim_of = {}
    for bit in range(sims_bits):
        dim_of[("sims", bit)] = sims_bits - 1 - bit
    for bit in range(sites_bits):
        dim_of[("sites", bit)] = total_bits - 1 - bit
    order = [("sims", 0), ("sims", sims_bits - 1)]
    pending = [("sims", b) for b in range(1, sims_bits - 1)]
    pending_sites = [("sites", b) for b in (2, 3, 0, 1) if b < sites_bits]
    pending_sites += [("sites", b) for b in range(sites_bits) if ("sites", b) not in pending_sites]
    while pending or pending_sites:
        if pending:
            order.append(pending.pop(0))
        if pending_sites:
            order.append(pending_sites.pop(0))
    order = list(dict.fromkeys(order))
    cells = flat.reshape((2,) * total_bits + (chunk // 512, 512))
    cells = cells.transpose([dim_of[o] for o in order] + [total_bits, total_bits + 1])
    current = cells.reshape(-1)
    return butterfly_kernel(current, small, order, chunk)


LANES = 256


def butterfly_body(order, steps_rows, small_rows, big_ref, small_ref, out_ref, small_out_ref,
                   acc, small_acc, recv, small_recv, send_sems, recv_sems, small_send_sems,
                   small_recv_sems):
    me = {"sims": lax.axis_index("sims"), "sites": lax.axis_index("sites")}
    partners = []
    for axis, bit in order:
        step = 1 << bit
        mine = (me[axis] // step) % 2
        other = dict(me)
        other[axis] = me[axis] + (1 - 2 * mine) * step
        partners.append(((other["sims"], other["sites"]), mine))
    barrier = pltpu.get_barrier_semaphore()
    for device, _ in partners:
        pl.semaphore_signal(barrier, inc=1, device_id=device, device_id_type=pl.DeviceIdType.MESH)
    pl.semaphore_wait(barrier, len(partners))
    acc[...] = big_ref[...]
    small_acc[...] = small_ref[...]
    base = 0
    lower = 0
    for k, ((device, mine), rows) in enumerate(zip(partners, steps_rows)):
        keep = pl.multiple_of(base + mine * rows, 8)
        away = pl.multiple_of(base + (1 - mine) * rows, 8)
        big_copy = pltpu.make_async_remote_copy(
            src_ref=acc.at[pl.ds(away, rows)],
            dst_ref=recv.at[pl.ds(lower, rows)],
            send_sem=send_sems.at[k],
            recv_sem=recv_sems.at[k],
            device_id=device,
            device_id_type=pl.DeviceIdType.MESH,
        )
        small_copy = pltpu.make_async_remote_copy(
            src_ref=small_acc,
            dst_ref=small_recv.at[k],
            send_sem=small_send_sems.at[k],
            recv_sem=small_recv_sems.at[k],
            device_id=device,
            device_id_type=pl.DeviceIdType.MESH,
        )
        big_copy.start()
        small_copy.start()
        big_copy.wait_send()
        small_copy.wait_send()
        big_copy.wait_recv()
        small_copy.wait_recv()
        acc[pl.ds(keep, rows)] = acc[pl.ds(keep, rows)] + recv[pl.ds(lower, rows)]
        small_acc[...] = small_acc[...] + small_recv[k]
        base = keep
        lower += rows
    out_ref[...] = acc[pl.ds(pl.multiple_of(base, 8), steps_rows[-1])]
    small_out_ref[...] = small_acc[...]


def butterfly_kernel(current, small, order, chunk):
    size = small.shape[0]
    small_rows = -(-size // (LANES * 8)) * 8
    small_grid = jnp.pad(small, (0, small_rows * LANES - size)).reshape(small_rows, LANES)
    big_rows = current.shape[0] // LANES
    steps_rows = [big_rows >> (k + 1) for k in range(len(order))]
    f32 = jnp.float32
    out, small_out = pl.pallas_call(
        functools.partial(butterfly_body, order, steps_rows, small_rows),
        out_shape=(
            jax.ShapeDtypeStruct((steps_rows[-1], LANES), f32),
            jax.ShapeDtypeStruct((small_rows, LANES), f32),
        ),
        in_specs=[pl.BlockSpec(memory_space=pltpu.VMEM)] * 2,
        out_specs=(pl.BlockSpec(memory_space=pltpu.VMEM),) * 2,
        scratch_shapes=[
            pltpu.VMEM((big_rows, LANES), f32),
            pltpu.VMEM((small_rows, LANES), f32),
            pltpu.VMEM((sum(steps_rows), LANES), f32),
            pltpu.VMEM((len(order), small_rows, LANES), f32),
            pltpu.SemaphoreType.DMA((len(order),)),
            pltpu.SemaphoreType.DMA((len(order),)),
            pltpu.SemaphoreType.DMA((len(order),)),
            pltpu.SemaphoreType.DMA((len(order),)),
        ],
        compiler_params=pltpu.CompilerParams(
            collective_id=0, has_side_effects=True, vmem_limit_bytes=48 * 1024 * 1024
        ),
    )(current.reshape(big_rows, LANES), small_grid)
    return out.reshape(chunk), small_out.reshape(-1)[:size]

def per_device(
    genotypes,
    key_prior,
    band_reach,
    cotangent,
    conv_weight,
    conv_bias,
    mix_weight,
    embed_weight,
    norm_gain,
    attn_weight,
):
    sims, haps, sites = genotypes.shape
    patch = conv_weight.shape[0]
    local = sites // patch
    width = attn_weight.shape[1]
    heads = HEADS
    factor = HEAD_DIM ** (-0.5)
    count = lax.axis_size("sites")
    cycle_tokens = local * count
    place = lax.axis_index("sites")
    ordinal = jnp.arange(local, dtype=jnp.int32)
    patches = genotypes.astype(jnp.float32).reshape(sims, haps, local, patch)
    pre = (
        jnp.einsum("shtk,kc->shct", patches, conv_weight, precision=HIGH)
        + conv_bias[None, None, :, None]
    )
    pooled = jnp.mean(jax.nn.silu(pre), axis=1)
    pooled_wide = extended(pooled, (("sites", 2),), 1)
    mixed = jnp.zeros((sims, mix_weight.shape[2], local), jnp.float32)
    for shift_by in (-1, 0, 1):
        mixed = mixed + jnp.einsum(
            "co,sct->sot",
            mix_weight[shift_by + 1],
            pooled_wide[:, :, 1 + shift_by : 1 + shift_by + local],
            precision=HIGH,
        )
    activated = jax.nn.silu(mixed)
    embedded = jnp.einsum("sct,cd->std", activated, embed_weight, precision=HIGH).astype(
        jnp.bfloat16
    )
    wide = embedded.astype(jnp.float32)
    inverse = lax.rsqrt(jnp.mean(wide * wide, axis=2, keepdims=True) + EPS)
    normed = (wide * inverse * norm_gain).astype(jnp.bfloat16)
    query = jnp.einsum(
        "std,de->ste", normed, attn_weight[0], preferred_element_type=jnp.float32
    ).astype(jnp.bfloat16)
    keys = jnp.einsum(
        "std,de->ste", normed, attn_weight[1], preferred_element_type=jnp.float32
    ).astype(jnp.bfloat16)
    values = jnp.einsum(
        "std,de->ste", normed, attn_weight[2], preferred_element_type=jnp.float32
    ).astype(jnp.bfloat16)
    query_heads = split_heads(query, heads)
    key_heads = split_heads(keys, heads)
    value_heads = split_heads(values, heads)
    reach_blocks = -(-BAND // local)
    offsets = block_offsets(count, reach_blocks)
    packed = jnp.concatenate(
        [keys, values, key_prior[:, :, None]], axis=2
    )
    gathered = {0: packed}
    for offset in offsets[1:]:
        gathered[offset] = from_behind(packed, "sites", -offset)
    packed_cat = jnp.concatenate([gathered[offset] for offset in offsets], axis=1)
    key_cat = split_heads(packed_cat[:, :, :width], heads)
    value_cat = split_heads(packed_cat[:, :, width : 2 * width], heads)
    prior_cat = packed_cat[:, :, 2 * width]
    key_places = jnp.concatenate([(place + offset) % count * local + ordinal for offset in offsets])
    query_places = place * local + ordinal
    scores, inside = band_scores(
        query_heads, key_cat, prior_cat, query_places, key_places, band_reach, cycle_tokens, factor
    )
    row_top = jnp.max(jnp.where(inside, scores, -jnp.inf), axis=-1, keepdims=True)
    lifted = jnp.where(inside, jnp.exp(scores - row_top), 0.0)
    row_total = jnp.sum(lifted, axis=-1, keepdims=True)
    prob = lifted / row_total
    prob_half = prob.astype(jnp.bfloat16)
    attended_full = jnp.einsum(
        "shqk,skhe->sqhe", prob_half, value_cat, preferred_element_type=jnp.float32
    )
    attended = attended_full.astype(jnp.bfloat16).reshape(sims, local, width)
    grad_attended = jnp.einsum(
        "std,ed->ste", cotangent, attn_weight[3], preferred_element_type=jnp.float32
    ).astype(jnp.bfloat16)
    grad_heads = split_heads(grad_attended, heads)
    delta = jnp.einsum("sqhe,sqhe->shq", grad_heads.astype(jnp.float32), attended_full)
    grad_prob = jnp.einsum(
        "sqhe,skhe->shqk", grad_heads, value_cat, preferred_element_type=jnp.float32
    )
    grad_scores = (prob * (grad_prob - delta[..., None]) * factor).astype(jnp.bfloat16)
    grad_query = jnp.einsum(
        "shqk,skhe->sqhe", grad_scores, key_cat, preferred_element_type=jnp.float32
    ).astype(jnp.bfloat16)
    grad_query = grad_query.reshape(sims, local, width)
    key_part = jnp.einsum(
        "shqk,sqhe->skhe", grad_scores, query_heads, preferred_element_type=jnp.float32
    )
    value_part = jnp.einsum(
        "shqk,sqhe->skhe", prob_half, grad_heads, preferred_element_type=jnp.float32
    )
    key_sum = key_part[:, 0:local]
    value_sum = value_part[:, 0:local]
    for position, offset in enumerate(offsets[1:], start=1):
        lower = position * local
        both = jnp.concatenate(
            [key_part[:, lower : lower + local], value_part[:, lower : lower + local]], axis=2
        ).astype(jnp.bfloat16)
        back = from_behind(both, "sites", offset).astype(jnp.float32)
        key_sum = key_sum + back[:, :, :heads]
        value_sum = value_sum + back[:, :, heads:]
    grad_keys = key_sum.astype(jnp.bfloat16).reshape(sims, local, width)
    grad_values = value_sum.astype(jnp.bfloat16).reshape(sims, local, width)
    term_query = jnp.einsum("std,ste->de", normed, grad_query, preferred_element_type=jnp.float32)
    term_keys = jnp.einsum("std,ste->de", normed, grad_keys, preferred_element_type=jnp.float32)
    term_values = jnp.einsum("std,ste->de", normed, grad_values, preferred_element_type=jnp.float32)
    term_output = jnp.einsum("std,ste->de", attended, cotangent, preferred_element_type=jnp.float32)
    flat_terms = jnp.stack([term_query, term_keys, term_values, term_output]).reshape(-1)
    grad_normed = jnp.einsum(
        "ste,de->std", grad_query, attn_weight[0], preferred_element_type=jnp.float32
    )
    grad_normed = grad_normed + jnp.einsum(
        "ste,de->std", grad_keys, attn_weight[1], preferred_element_type=jnp.float32
    )
    grad_normed = grad_normed + jnp.einsum(
        "ste,de->std", grad_values, attn_weight[2], preferred_element_type=jnp.float32
    )
    term_gain = jnp.sum(grad_normed * wide * inverse, axis=(0, 1))
    scaled = grad_normed * norm_gain
    grad_embedded = (
        inverse * scaled - wide * inverse**3 * jnp.sum(scaled * wide, axis=2, keepdims=True) / width
    )
    grad_embedded = grad_embedded + cotangent.astype(jnp.float32)
    term_embed = jnp.einsum("sct,std->cd", activated, grad_embedded, precision=HIGH)
    grad_mixed = jnp.einsum(
        "std,od->sot", grad_embedded, embed_weight, precision=HIGH
    ) * silu_slope(mixed)
    mixed_wide = extended(grad_mixed.astype(jnp.bfloat16), (("sites", 2),), 1).astype(
        grad_mixed.dtype
    )
    mix_terms = []
    grad_pooled = jnp.zeros(pooled.shape, jnp.float32)
    for shift_by in (-1, 0, 1):
        mix_terms.append(
            jnp.einsum(
                "sct,sot->co",
                pooled_wide[:, :, 1 + shift_by : 1 + shift_by + local],
                grad_mixed,
                precision=HIGH,
            )
        )
        grad_pooled = grad_pooled + jnp.einsum(
            "co,sot->sct",
            mix_weight[shift_by + 1],
            mixed_wide[:, :, 1 - shift_by : 1 - shift_by + local],
            precision=HIGH,
        )
    grad_pre = (grad_pooled / haps)[:, None] * silu_slope(pre)
    term_conv = jnp.einsum("shtk,shct->kc", patches, grad_pre, precision=HIGH)
    term_bias = jnp.sum(grad_pre, axis=(0, 1, 3))
    small = (term_conv, term_bias, jnp.stack(mix_terms), term_embed, term_gain)
    flat_small = jnp.concatenate([t.reshape(-1) for t in small])
    grad_attention, flat_small = butterfly_sum(flat_terms, flat_small)
    pieces = []
    lower = 0
    for t in small:
        pieces.append(flat_small[lower : lower + t.size].reshape(t.shape))
        lower += t.size
    grad_conv, grad_bias, grad_mix, grad_embed, grad_gain = pieces
    return (grad_attention, grad_conv, grad_bias, grad_mix, grad_embed, grad_gain)


def solution(mesh):
    placed = (
        P("sims", None, "sites"),
        P("sims", "sites"),
        P("sims"),
        P("sims", "sites", None),
        P(),
        P(),
        P(),
        P(),
        P(),
        P(),
    )
    return jax.shard_map(
        per_device,
        mesh=mesh,
        in_specs=placed,
        out_specs=(P(("sims", "sites")), P(), P(), P(), P(), P()),
        check_vma=False,
    )
```

```python
import functools

import jax
import jax.numpy as jnp
from jax import lax
from jax.experimental import pallas as pl
from jax.experimental.pallas import tpu as pltpu
from jax.sharding import PartitionSpec as P

HEADS = 8
HEAD_DIM = 64
BAND = 512


HIGH = lax.Precision.HIGHEST
EPS = 1e-06


def extended(cells, sides, width):
    for axis, dim in sides:
        count = lax.axis_size(axis)
        head = lax.slice_in_dim(cells, 0, width, axis=dim)
        tail = lax.slice_in_dim(cells, cells.shape[dim] - width, cells.shape[dim], axis=dim)
        cells = jnp.concatenate(
            [
                lax.ppermute(tail, axis, [(i, (i + 1) % count) for i in range(count)]),
                cells,
                lax.ppermute(head, axis, [((i + 1) % count, i) for i in range(count)]),
            ],
            axis=dim,
        )
    return cells


def from_behind(value, axis, steps):
    count = lax.axis_size(axis)
    pairs = [(source, (source + steps) % count) for source in range(count)]
    return lax.ppermute(value, axis, pairs)


def silu_slope(value):
    sigma = jax.nn.sigmoid(value)
    return sigma * (1.0 + value * (1.0 - sigma))


def block_offsets(count, reach_blocks):
    chosen = []
    taken = []
    for distance in range(reach_blocks + 1):
        for offset in (distance, -distance):
            if offset % count not in taken:
                taken.append(offset % count)
                chosen.append(offset)
    return chosen


def split_heads(array, heads):
    return array.reshape(array.shape[0], array.shape[1], heads, array.shape[2] // heads)


def band_scores(query, keys, prior, query_places, key_places, limit, cycle_tokens, factor):
    scores = jnp.einsum("sqhe,skhe->shqk", query, keys, preferred_element_type=jnp.float32) * factor
    scores = scores + prior.astype(jnp.float32)[:, None, None, :]
    apart = (key_places[None, :] - query_places[:, None]) % cycle_tokens
    apart = jnp.minimum(apart, cycle_tokens - apart)
    inside = apart[None, None] <= limit[:, None, None, None]
    return (scores, inside)


def bit_count(size):
    bits = size.bit_length() - 1
    assert 1 << bits == size
    return bits


def butterfly_sum(flat, small):
    sims_bits = bit_count(lax.axis_size("sims"))
    sites_bits = bit_count(lax.axis_size("sites"))
    total_bits = sims_bits + sites_bits
    chunk = flat.shape[0] >> total_bits
    dim_of = {}
    for bit in range(sims_bits):
        dim_of[("sims", bit)] = sims_bits - 1 - bit
    for bit in range(sites_bits):
        dim_of[("sites", bit)] = total_bits - 1 - bit
    order = [("sims", 0), ("sims", sims_bits - 1)]
    pending = [("sims", b) for b in range(1, sims_bits - 1)]
    pending_sites = [("sites", b) for b in (2, 3, 0, 1) if b < sites_bits]
    pending_sites += [("sites", b) for b in range(sites_bits) if ("sites", b) not in pending_sites]
    while pending or pending_sites:
        if pending:
            order.append(pending.pop(0))
        if pending_sites:
            order.append(pending_sites.pop(0))
    order = list(dict.fromkeys(order))
    cells = flat.reshape((2,) * total_bits + (chunk // LANES, LANES))
    cells = cells.transpose([dim_of[o] for o in order] + [total_bits, total_bits + 1])
    current = cells.reshape(-1, LANES)
    small_order = order[3:4] + order[2:3] + order[1:2] + order[0:1] + order[5:6] + order[4:5]
    small_order += order[8:9] + order[6:7] + order[7:8]
    small_order += [o for o in order if o not in small_order]
    small_order = list(dict.fromkeys(small_order))
    return butterfly_kernel(current, small, order, small_order, chunk)


LANES = 256


def butterfly_body(order, small_order, steps_rows, small_rows, big_ref, small_ref, out_ref, small_out_ref,
                   acc, small_acc, recv, small_recv, send_sems, recv_sems, small_send_sems,
                   small_recv_sems):
    me = {"sims": lax.axis_index("sims"), "sites": lax.axis_index("sites")}
    def partner(axis, bit):
        step = 1 << bit
        mine = (me[axis] // step) % 2
        other = dict(me)
        other[axis] = me[axis] + (1 - 2 * mine) * step
        return ((other["sims"], other["sites"]), mine)

    partners = [partner(axis, bit) for axis, bit in order]
    small_partners = [partner(axis, bit)[0] for axis, bit in small_order]
    barrier = pltpu.get_barrier_semaphore()
    for device, _ in partners:
        pl.semaphore_signal(barrier, inc=1, device_id=device, device_id_type=pl.DeviceIdType.MESH)
    pl.semaphore_wait(barrier, len(partners))
    acc[...] = big_ref[...]
    small_acc[...] = small_ref[...]
    base = 0
    lower = 0
    for k, ((device, mine), rows) in enumerate(zip(partners, steps_rows)):
        keep = pl.multiple_of(base + mine * rows, 8)
        away = pl.multiple_of(base + (1 - mine) * rows, 8)
        big_copy = pltpu.make_async_remote_copy(
            src_ref=acc.at[pl.ds(away, rows)],
            dst_ref=recv.at[pl.ds(lower, rows)],
            send_sem=send_sems.at[k],
            recv_sem=recv_sems.at[k],
            device_id=device,
            device_id_type=pl.DeviceIdType.MESH,
        )
        small_copy = pltpu.make_async_remote_copy(
            src_ref=small_acc,
            dst_ref=small_recv.at[k],
            send_sem=small_send_sems.at[k],
            recv_sem=small_recv_sems.at[k],
            device_id=small_partners[k],
            device_id_type=pl.DeviceIdType.MESH,
        )
        big_copy.start()
        small_copy.start()
        big_copy.wait_send()
        small_copy.wait_send()
        big_copy.wait_recv()
        small_copy.wait_recv()
        acc[pl.ds(keep, rows)] = acc[pl.ds(keep, rows)] + recv[pl.ds(lower, rows)]
        small_acc[...] = small_acc[...] + small_recv[k]
        base = keep
        lower += rows
    out_ref[...] = acc[pl.ds(pl.multiple_of(base, 8), steps_rows[-1])]
    small_out_ref[...] = small_acc[...]


def butterfly_kernel(current, small, order, small_order, chunk):
    size = small.shape[0]
    small_rows = -(-size // (LANES * 8)) * 8
    small_grid = jnp.pad(small, (0, small_rows * LANES - size)).reshape(small_rows, LANES)
    big_rows = current.shape[0]
    steps_rows = [big_rows >> (k + 1) for k in range(len(order))]
    f32 = jnp.float32
    out, small_out = pl.pallas_call(
        functools.partial(butterfly_body, order, small_order, steps_rows, small_rows),
        out_shape=(
            jax.ShapeDtypeStruct((steps_rows[-1], LANES), f32),
            jax.ShapeDtypeStruct((small_rows, LANES), f32),
        ),
        in_specs=[pl.BlockSpec(memory_space=pltpu.VMEM)] * 2,
        out_specs=(pl.BlockSpec(memory_space=pltpu.VMEM),) * 2,
        scratch_shapes=[
            pltpu.VMEM((big_rows, LANES), f32),
            pltpu.VMEM((small_rows, LANES), f32),
            pltpu.VMEM((sum(steps_rows), LANES), f32),
            pltpu.VMEM((len(order), small_rows, LANES), f32),
            pltpu.SemaphoreType.DMA((len(order),)),
            pltpu.SemaphoreType.DMA((len(order),)),
            pltpu.SemaphoreType.DMA((len(order),)),
            pltpu.SemaphoreType.DMA((len(order),)),
        ],
        compiler_params=pltpu.CompilerParams(
            collective_id=0, has_side_effects=True, vmem_limit_bytes=48 * 1024 * 1024
        ),
    )(current, small_grid)
    return out.reshape(chunk), small_out.reshape(-1)[:size]

def per_device(
    genotypes,
    key_prior,
    band_reach,
    cotangent,
    conv_weight,
    conv_bias,
    mix_weight,
    embed_weight,
    norm_gain,
    attn_weight,
):
    sims, haps, sites = genotypes.shape
    patch = conv_weight.shape[0]
    local = sites // patch
    width = attn_weight.shape[1]
    heads = HEADS
    factor = HEAD_DIM ** (-0.5)
    count = lax.axis_size("sites")
    cycle_tokens = local * count
    place = lax.axis_index("sites")
    ordinal = jnp.arange(local, dtype=jnp.int32)
    patches = genotypes.astype(jnp.float32).reshape(sims, haps, local, patch)
    pre = (
        jnp.einsum("shtk,kc->shct", patches, conv_weight, precision=HIGH)
        + conv_bias[None, None, :, None]
    )
    pooled = jnp.mean(jax.nn.silu(pre), axis=1)
    pooled_wide = extended(pooled, (("sites", 2),), 1)
    mixed = jnp.zeros((sims, mix_weight.shape[2], local), jnp.float32)
    for shift_by in (-1, 0, 1):
        mixed = mixed + jnp.einsum(
            "co,sct->sot",
            mix_weight[shift_by + 1],
            pooled_wide[:, :, 1 + shift_by : 1 + shift_by + local],
            precision=HIGH,
        )
    activated = jax.nn.silu(mixed)
    embedded = jnp.einsum("sct,cd->std", activated, embed_weight, precision=HIGH).astype(
        jnp.bfloat16
    )
    wide = embedded.astype(jnp.float32)
    inverse = lax.rsqrt(jnp.mean(wide * wide, axis=2, keepdims=True) + EPS)
    normed = (wide * inverse * norm_gain).astype(jnp.bfloat16)
    query = jnp.einsum(
        "std,de->ste", normed, attn_weight[0], preferred_element_type=jnp.float32
    ).astype(jnp.bfloat16)
    keys = jnp.einsum(
        "std,de->ste", normed, attn_weight[1], preferred_element_type=jnp.float32
    ).astype(jnp.bfloat16)
    values = jnp.einsum(
        "std,de->ste", normed, attn_weight[2], preferred_element_type=jnp.float32
    ).astype(jnp.bfloat16)
    query_heads = split_heads(query, heads)
    key_heads = split_heads(keys, heads)
    value_heads = split_heads(values, heads)
    reach_blocks = -(-BAND // local)
    offsets = block_offsets(count, reach_blocks)
    packed = jnp.concatenate(
        [keys, values, key_prior[:, :, None]], axis=2
    )
    gathered = {0: packed}
    for offset in offsets[1:]:
        gathered[offset] = from_behind(packed, "sites", -offset)
    packed_cat = jnp.concatenate([gathered[offset] for offset in offsets], axis=1)
    key_cat = split_heads(packed_cat[:, :, :width], heads)
    value_cat = split_heads(packed_cat[:, :, width : 2 * width], heads)
    prior_cat = packed_cat[:, :, 2 * width]
    key_places = jnp.concatenate([(place + offset) % count * local + ordinal for offset in offsets])
    query_places = place * local + ordinal
    scores, inside = band_scores(
        query_heads, key_cat, prior_cat, query_places, key_places, band_reach, cycle_tokens, factor
    )
    row_top = jnp.max(jnp.where(inside, scores, -jnp.inf), axis=-1, keepdims=True)
    lifted = jnp.where(inside, jnp.exp(scores - row_top), 0.0)
    row_total = jnp.sum(lifted, axis=-1, keepdims=True)
    prob = lifted / row_total
    prob_half = prob.astype(jnp.bfloat16)
    attended_full = jnp.einsum(
        "shqk,skhe->sqhe", prob_half, value_cat, preferred_element_type=jnp.float32
    )
    attended = attended_full.astype(jnp.bfloat16).reshape(sims, local, width)
    grad_attended = jnp.einsum(
        "std,ed->ste", cotangent, attn_weight[3], preferred_element_type=jnp.float32
    ).astype(jnp.bfloat16)
    grad_heads = split_heads(grad_attended, heads)
    delta = jnp.einsum("sqhe,sqhe->shq", grad_heads.astype(jnp.float32), attended_full)
    grad_prob = jnp.einsum(
        "sqhe,skhe->shqk", grad_heads, value_cat, preferred_element_type=jnp.float32
    )
    grad_scores = (prob * (grad_prob - delta[..., None]) * factor).astype(jnp.bfloat16)
    grad_query = jnp.einsum(
        "shqk,skhe->sqhe", grad_scores, key_cat, preferred_element_type=jnp.float32
    ).astype(jnp.bfloat16)
    grad_query = grad_query.reshape(sims, local, width)
    key_part = jnp.einsum(
        "shqk,sqhe->skhe", grad_scores, query_heads, preferred_element_type=jnp.float32
    )
    value_part = jnp.einsum(
        "shqk,sqhe->skhe", prob_half, grad_heads, preferred_element_type=jnp.float32
    )
    key_sum = key_part[:, 0:local]
    value_sum = value_part[:, 0:local]
    for position, offset in enumerate(offsets[1:], start=1):
        lower = position * local
        both = jnp.concatenate(
            [key_part[:, lower : lower + local], value_part[:, lower : lower + local]], axis=2
        ).astype(jnp.bfloat16)
        back = from_behind(both, "sites", offset).astype(jnp.float32)
        key_sum = key_sum + back[:, :, :heads]
        value_sum = value_sum + back[:, :, heads:]
    grad_keys = key_sum.astype(jnp.bfloat16).reshape(sims, local, width)
    grad_values = value_sum.astype(jnp.bfloat16).reshape(sims, local, width)
    term_query = jnp.einsum("std,ste->de", normed, grad_query, preferred_element_type=jnp.float32)
    term_keys = jnp.einsum("std,ste->de", normed, grad_keys, preferred_element_type=jnp.float32)
    term_values = jnp.einsum("std,ste->de", normed, grad_values, preferred_element_type=jnp.float32)
    term_output = jnp.einsum("std,ste->de", attended, cotangent, preferred_element_type=jnp.float32)
    flat_terms = jnp.stack([term_query, term_keys, term_values, term_output]).reshape(-1)
    grad_normed = jnp.einsum(
        "ste,de->std", grad_query, attn_weight[0], preferred_element_type=jnp.float32
    )
    grad_normed = grad_normed + jnp.einsum(
        "ste,de->std", grad_keys, attn_weight[1], preferred_element_type=jnp.float32
    )
    grad_normed = grad_normed + jnp.einsum(
        "ste,de->std", grad_values, attn_weight[2], preferred_element_type=jnp.float32
    )
    term_gain = jnp.sum(grad_normed * wide * inverse, axis=(0, 1))
    scaled = grad_normed * norm_gain
    grad_embedded = (
        inverse * scaled - wide * inverse**3 * jnp.sum(scaled * wide, axis=2, keepdims=True) / width
    )
    grad_embedded = grad_embedded + cotangent.astype(jnp.float32)
    term_embed = jnp.einsum("sct,std->cd", activated, grad_embedded, precision=HIGH)
    grad_mixed = jnp.einsum(
        "std,od->sot", grad_embedded, embed_weight, precision=HIGH
    ) * silu_slope(mixed)
    mixed_wide = extended(grad_mixed.astype(jnp.bfloat16), (("sites", 2),), 1).astype(
        grad_mixed.dtype
    )
    mix_terms = []
    grad_pooled = jnp.zeros(pooled.shape, jnp.float32)
    for shift_by in (-1, 0, 1):
        mix_terms.append(
            jnp.einsum(
                "sct,sot->co",
                pooled_wide[:, :, 1 + shift_by : 1 + shift_by + local],
                grad_mixed,
                precision=HIGH,
            )
        )
        grad_pooled = grad_pooled + jnp.einsum(
            "co,sot->sct",
            mix_weight[shift_by + 1],
            mixed_wide[:, :, 1 - shift_by : 1 - shift_by + local],
            precision=HIGH,
        )
    grad_pre = (grad_pooled / haps)[:, None] * silu_slope(pre)
    term_conv = jnp.einsum("shtk,shct->kc", patches, grad_pre, precision=HIGH)
    term_bias = jnp.sum(grad_pre, axis=(0, 1, 3))
    small = (term_conv, term_bias, jnp.stack(mix_terms), term_embed, term_gain)
    flat_small = jnp.concatenate([t.reshape(-1) for t in small])
    grad_attention, flat_small = butterfly_sum(flat_terms, flat_small)
    pieces = []
    lower = 0
    for t in small:
        pieces.append(flat_small[lower : lower + t.size].reshape(t.shape))
        lower += t.size
    grad_conv, grad_bias, grad_mix, grad_embed, grad_gain = pieces
    return (grad_attention, grad_conv, grad_bias, grad_mix, grad_embed, grad_gain)


def solution(mesh):
    placed = (
        P("sims", None, "sites"),
        P("sims", "sites"),
        P("sims"),
        P("sims", "sites", None),
        P(),
        P(),
        P(),
        P(),
        P(),
        P(),
    )
    return jax.shard_map(
        per_device,
        mesh=mesh,
        in_specs=placed,
        out_specs=(P(("sims", "sites")), P(), P(), P(), P(), P()),
        check_vma=False,
    )
```

```python
import functools

import jax
import jax.numpy as jnp
from jax import lax
from jax.experimental import pallas as pl
from jax.experimental.pallas import tpu as pltpu
from jax.sharding import PartitionSpec as P

HEADS = 8
HEAD_DIM = 64
BAND = 512


HIGH = lax.Precision.HIGHEST
EPS = 1e-06


def extended(cells, sides, width):
    for axis, dim in sides:
        count = lax.axis_size(axis)
        head = lax.slice_in_dim(cells, 0, width, axis=dim)
        tail = lax.slice_in_dim(cells, cells.shape[dim] - width, cells.shape[dim], axis=dim)
        cells = jnp.concatenate(
            [
                lax.ppermute(tail, axis, [(i, (i + 1) % count) for i in range(count)]),
                cells,
                lax.ppermute(head, axis, [((i + 1) % count, i) for i in range(count)]),
            ],
            axis=dim,
        )
    return cells


def from_behind(value, axis, steps):
    count = lax.axis_size(axis)
    pairs = [(source, (source + steps) % count) for source in range(count)]
    return lax.ppermute(value, axis, pairs)


def silu_slope(value):
    sigma = jax.nn.sigmoid(value)
    return sigma * (1.0 + value * (1.0 - sigma))


def block_offsets(count, reach_blocks):
    chosen = []
    taken = []
    for distance in range(reach_blocks + 1):
        for offset in (distance, -distance):
            if offset % count not in taken:
                taken.append(offset % count)
                chosen.append(offset)
    return chosen


def split_heads(array, heads):
    return array.reshape(array.shape[0], array.shape[1], heads, array.shape[2] // heads)


def band_scores(query, keys, prior, query_places, key_places, limit, cycle_tokens, factor):
    scores = jnp.einsum("sqhe,skhe->shqk", query, keys, preferred_element_type=jnp.float32) * factor
    scores = scores + prior.astype(jnp.float32)[:, None, None, :]
    apart = (key_places[None, :] - query_places[:, None]) % cycle_tokens
    apart = jnp.minimum(apart, cycle_tokens - apart)
    inside = apart[None, None] <= limit[:, None, None, None]
    return (scores, inside)


def bit_count(size):
    bits = size.bit_length() - 1
    assert 1 << bits == size
    return bits


def butterfly_sum(flat, small):
    sims_bits = bit_count(lax.axis_size("sims"))
    sites_bits = bit_count(lax.axis_size("sites"))
    total_bits = sims_bits + sites_bits
    chunk = flat.shape[0] >> total_bits
    dim_of = {}
    for bit in range(sims_bits):
        dim_of[("sims", bit)] = sims_bits - 1 - bit
    for bit in range(sites_bits):
        dim_of[("sites", bit)] = total_bits - 1 - bit
    order = [("sims", 0), ("sims", sims_bits - 1)]
    pending = [("sims", b) for b in range(1, sims_bits - 1)]
    pending_sites = [("sites", b) for b in (2, 3, 0, 1) if b < sites_bits]
    pending_sites += [("sites", b) for b in range(sites_bits) if ("sites", b) not in pending_sites]
    while pending or pending_sites:
        if pending:
            order.append(pending.pop(0))
        if pending_sites:
            order.append(pending_sites.pop(0))
    order = list(dict.fromkeys(order))
    cells = flat.reshape((2,) * total_bits + (chunk // LANES, LANES))
    cells = cells.transpose([dim_of[o] for o in order] + [total_bits, total_bits + 1])
    current = cells.reshape(-1, LANES)
    small_order = order[3:4] + order[2:3] + order[1:2] + order[0:1] + order[5:6] + order[4:5]
    small_order += order[8:9] + order[6:7] + order[7:8]
    small_order += [o for o in order if o not in small_order]
    small_order = list(dict.fromkeys(small_order))
    return butterfly_kernel(current, small, order, small_order, chunk)


LANES = 256


def butterfly_body(order, small_order, steps_rows, small_rows, big_ref, small_ref, out_ref, small_out_ref,
                   acc, small_acc, recv, small_recv, send_sems, recv_sems, small_send_sems,
                   small_recv_sems):
    me = {"sims": lax.axis_index("sims"), "sites": lax.axis_index("sites")}
    def partner(axis, bit):
        step = 1 << bit
        mine = (me[axis] // step) % 2
        other = dict(me)
        other[axis] = me[axis] + (1 - 2 * mine) * step
        return ((other["sims"], other["sites"]), mine)

    partners = [partner(axis, bit) for axis, bit in order]
    small_partners = [partner(axis, bit)[0] for axis, bit in small_order]
    barrier = pltpu.get_barrier_semaphore()
    for device, _ in partners:
        pl.semaphore_signal(barrier, inc=1, device_id=device, device_id_type=pl.DeviceIdType.MESH)
    pl.semaphore_wait(barrier, len(partners))
    acc[...] = big_ref[...]
    small_acc[...] = small_ref[...]
    base = 0
    lower = 0
    for k, ((device, mine), rows) in enumerate(zip(partners, steps_rows)):
        keep = pl.multiple_of(base + mine * rows, 8)
        away = pl.multiple_of(base + (1 - mine) * rows, 8)
        big_copy = pltpu.make_async_remote_copy(
            src_ref=acc.at[pl.ds(away, rows)],
            dst_ref=recv.at[pl.ds(lower, rows)],
            send_sem=send_sems.at[k],
            recv_sem=recv_sems.at[k],
            device_id=device,
            device_id_type=pl.DeviceIdType.MESH,
        )
        small_copy = pltpu.make_async_remote_copy(
            src_ref=small_acc,
            dst_ref=small_recv.at[k],
            send_sem=small_send_sems.at[k],
            recv_sem=small_recv_sems.at[k],
            device_id=small_partners[k],
            device_id_type=pl.DeviceIdType.MESH,
        )
        big_copy.start()
        small_copy.start()
        big_copy.wait_send()
        small_copy.wait_send()
        big_copy.wait_recv()
        small_copy.wait_recv()
        acc[pl.ds(keep, rows)] = acc[pl.ds(keep, rows)] + recv[pl.ds(lower, rows)]
        small_acc[...] = small_acc[...] + small_recv[k]
        base = keep
        lower += rows
    out_ref[...] = acc[pl.ds(pl.multiple_of(base, 8), steps_rows[-1])]
    small_out_ref[...] = small_acc[...]


def butterfly_kernel(current, small, order, small_order, chunk):
    size = small.shape[0]
    small_rows = -(-size // (LANES * 8)) * 8
    small_grid = jnp.pad(small, (0, small_rows * LANES - size)).reshape(small_rows, LANES)
    big_rows = current.shape[0]
    steps_rows = [big_rows >> (k + 1) for k in range(len(order))]
    f32 = jnp.float32
    out, small_out = pl.pallas_call(
        functools.partial(butterfly_body, order, small_order, steps_rows, small_rows),
        out_shape=(
            jax.ShapeDtypeStruct((steps_rows[-1], LANES), f32),
            jax.ShapeDtypeStruct((small_rows, LANES), f32),
        ),
        in_specs=[pl.BlockSpec(memory_space=pltpu.VMEM)] * 2,
        out_specs=(pl.BlockSpec(memory_space=pltpu.VMEM),) * 2,
        scratch_shapes=[
            pltpu.VMEM((big_rows, LANES), f32),
            pltpu.VMEM((small_rows, LANES), f32),
            pltpu.VMEM((sum(steps_rows), LANES), f32),
            pltpu.VMEM((len(order), small_rows, LANES), f32),
            pltpu.SemaphoreType.DMA((len(order),)),
            pltpu.SemaphoreType.DMA((len(order),)),
            pltpu.SemaphoreType.DMA((len(order),)),
            pltpu.SemaphoreType.DMA((len(order),)),
        ],
        compiler_params=pltpu.CompilerParams(
            collective_id=0, has_side_effects=True, vmem_limit_bytes=48 * 1024 * 1024
        ),
    )(current, small_grid)
    return out.reshape(chunk), small_out.reshape(-1)[:size]

def exchange_body(shifts, per_slot, src_ref, out_ref, held, send_sems, recv_sems):
    place = lax.axis_index("sites")
    row = lax.axis_index("sims")
    count = lax.axis_size("sites")
    targets = [(row, lax.rem(place + shift + count, count)) for shift in shifts]
    barrier = pltpu.get_barrier_semaphore()
    for device in targets:
        pl.semaphore_signal(barrier, inc=1, device_id=device, device_id_type=pl.DeviceIdType.MESH)
    pl.semaphore_wait(barrier, len(targets))
    copies = []
    for slot, device in enumerate(targets):
        copy = pltpu.make_async_remote_copy(
            src_ref=src_ref.at[slot] if per_slot else src_ref,
            dst_ref=held.at[slot],
            send_sem=send_sems.at[slot],
            recv_sem=recv_sems.at[slot],
            device_id=device,
            device_id_type=pl.DeviceIdType.MESH,
        )
        copy.start()
        copies.append(copy)
    for copy in copies:
        copy.wait_send()
    for copy in copies:
        copy.wait_recv()
    out_ref[...] = held[...]


def exchange(block, shifts, per_slot, collective):
    slots = len(shifts)
    shape = block.shape[1:] if per_slot else block.shape
    return pl.pallas_call(
        functools.partial(exchange_body, shifts, per_slot),
        out_shape=jax.ShapeDtypeStruct((slots,) + shape, block.dtype),
        in_specs=[pl.BlockSpec(memory_space=pltpu.VMEM)],
        out_specs=pl.BlockSpec(memory_space=pltpu.VMEM),
        scratch_shapes=[
            pltpu.VMEM((slots,) + shape, block.dtype),
            pltpu.SemaphoreType.DMA((slots,)),
            pltpu.SemaphoreType.DMA((slots,)),
        ],
        compiler_params=pltpu.CompilerParams(
            collective_id=collective, has_side_effects=True, vmem_limit_bytes=32 * 1024 * 1024
        ),
    )(block)


def per_device(
    genotypes,
    key_prior,
    band_reach,
    cotangent,
    conv_weight,
    conv_bias,
    mix_weight,
    embed_weight,
    norm_gain,
    attn_weight,
):
    sims, haps, sites = genotypes.shape
    patch = conv_weight.shape[0]
    local = sites // patch
    width = attn_weight.shape[1]
    heads = HEADS
    factor = HEAD_DIM ** (-0.5)
    count = lax.axis_size("sites")
    cycle_tokens = local * count
    place = lax.axis_index("sites")
    ordinal = jnp.arange(local, dtype=jnp.int32)
    patches = genotypes.astype(jnp.float32).reshape(sims, haps, local, patch)
    pre = (
        jnp.einsum("shtk,kc->shct", patches, conv_weight, precision=HIGH)
        + conv_bias[None, None, :, None]
    )
    pooled = jnp.mean(jax.nn.silu(pre), axis=1)
    pooled_wide = extended(pooled, (("sites", 2),), 1)
    mixed = jnp.zeros((sims, mix_weight.shape[2], local), jnp.float32)
    for shift_by in (-1, 0, 1):
        mixed = mixed + jnp.einsum(
            "co,sct->sot",
            mix_weight[shift_by + 1],
            pooled_wide[:, :, 1 + shift_by : 1 + shift_by + local],
            precision=HIGH,
        )
    activated = jax.nn.silu(mixed)
    embedded = jnp.einsum("sct,cd->std", activated, embed_weight, precision=HIGH).astype(
        jnp.bfloat16
    )
    wide = embedded.astype(jnp.float32)
    inverse = lax.rsqrt(jnp.mean(wide * wide, axis=2, keepdims=True) + EPS)
    normed = (wide * inverse * norm_gain).astype(jnp.bfloat16)
    query = jnp.einsum(
        "std,de->ste", normed, attn_weight[0], preferred_element_type=jnp.float32
    ).astype(jnp.bfloat16)
    keys = jnp.einsum(
        "std,de->ste", normed, attn_weight[1], preferred_element_type=jnp.float32
    ).astype(jnp.bfloat16)
    values = jnp.einsum(
        "std,de->ste", normed, attn_weight[2], preferred_element_type=jnp.float32
    ).astype(jnp.bfloat16)
    query_heads = split_heads(query, heads)
    key_heads = split_heads(keys, heads)
    value_heads = split_heads(values, heads)
    reach_blocks = -(-BAND // local)
    offsets = block_offsets(count, reach_blocks)
    packed = jnp.concatenate(
        [keys, values, key_prior[:, :, None]], axis=2
    )
    lane_pad = -packed.shape[2] % 128
    packed = jnp.pad(packed, ((0, 0), (0, 0), (0, lane_pad)))
    arrived = exchange(packed[0], [-offset for offset in offsets[1:]], False, 1)
    packed_cat = jnp.concatenate([packed[0][None], arrived], axis=0).reshape(
        1, len(offsets) * local, packed.shape[2]
    )
    key_cat = split_heads(packed_cat[:, :, :width], heads)
    value_cat = split_heads(packed_cat[:, :, width : 2 * width], heads)
    prior_cat = packed_cat[:, :, 2 * width]
    key_places = jnp.concatenate([(place + offset) % count * local + ordinal for offset in offsets])
    query_places = place * local + ordinal
    scores, inside = band_scores(
        query_heads, key_cat, prior_cat, query_places, key_places, band_reach, cycle_tokens, factor
    )
    row_top = jnp.max(jnp.where(inside, scores, -jnp.inf), axis=-1, keepdims=True)
    lifted = jnp.where(inside, jnp.exp(scores - row_top), 0.0)
    row_total = jnp.sum(lifted, axis=-1, keepdims=True)
    prob = lifted / row_total
    prob_half = prob.astype(jnp.bfloat16)
    attended_full = jnp.einsum(
        "shqk,skhe->sqhe", prob_half, value_cat, preferred_element_type=jnp.float32
    )
    attended = attended_full.astype(jnp.bfloat16).reshape(sims, local, width)
    grad_attended = jnp.einsum(
        "std,ed->ste", cotangent, attn_weight[3], preferred_element_type=jnp.float32
    ).astype(jnp.bfloat16)
    grad_heads = split_heads(grad_attended, heads)
    delta = jnp.einsum("sqhe,sqhe->shq", grad_heads.astype(jnp.float32), attended_full)
    grad_prob = jnp.einsum(
        "sqhe,skhe->shqk", grad_heads, value_cat, preferred_element_type=jnp.float32
    )
    grad_scores = (prob * (grad_prob - delta[..., None]) * factor).astype(jnp.bfloat16)
    grad_query = jnp.einsum(
        "shqk,skhe->sqhe", grad_scores, key_cat, preferred_element_type=jnp.float32
    ).astype(jnp.bfloat16)
    grad_query = grad_query.reshape(sims, local, width)
    key_part = jnp.einsum(
        "shqk,sqhe->skhe", grad_scores, query_heads, preferred_element_type=jnp.float32
    )
    value_part = jnp.einsum(
        "shqk,sqhe->skhe", prob_half, grad_heads, preferred_element_type=jnp.float32
    )
    key_sum = key_part[:, 0:local]
    value_sum = value_part[:, 0:local]
    parts = jnp.concatenate(
        [key_part[0, local:], value_part[0, local:]], axis=1
    ).astype(jnp.bfloat16).reshape(len(offsets) - 1, local, 2 * width)
    back = exchange(parts, list(offsets[1:]), True, 2).astype(jnp.float32)
    for position in range(len(offsets) - 1):
        key_sum = key_sum + back[position][None, :, :width].reshape(key_sum.shape)
        value_sum = value_sum + back[position][None, :, width:].reshape(value_sum.shape)
    grad_keys = key_sum.astype(jnp.bfloat16).reshape(sims, local, width)
    grad_values = value_sum.astype(jnp.bfloat16).reshape(sims, local, width)
    term_query = jnp.einsum("std,ste->de", normed, grad_query, preferred_element_type=jnp.float32)
    term_keys = jnp.einsum("std,ste->de", normed, grad_keys, preferred_element_type=jnp.float32)
    term_values = jnp.einsum("std,ste->de", normed, grad_values, preferred_element_type=jnp.float32)
    term_output = jnp.einsum("std,ste->de", attended, cotangent, preferred_element_type=jnp.float32)
    flat_terms = jnp.stack([term_query, term_keys, term_values, term_output]).reshape(-1)
    grad_normed = jnp.einsum(
        "ste,de->std", grad_query, attn_weight[0], preferred_element_type=jnp.float32
    )
    grad_normed = grad_normed + jnp.einsum(
        "ste,de->std", grad_keys, attn_weight[1], preferred_element_type=jnp.float32
    )
    grad_normed = grad_normed + jnp.einsum(
        "ste,de->std", grad_values, attn_weight[2], preferred_element_type=jnp.float32
    )
    term_gain = jnp.sum(grad_normed * wide * inverse, axis=(0, 1))
    scaled = grad_normed * norm_gain
    grad_embedded = (
        inverse * scaled - wide * inverse**3 * jnp.sum(scaled * wide, axis=2, keepdims=True) / width
    )
    grad_embedded = grad_embedded + cotangent.astype(jnp.float32)
    term_embed = jnp.einsum("sct,std->cd", activated, grad_embedded, precision=HIGH)
    grad_mixed = jnp.einsum(
        "std,od->sot", grad_embedded, embed_weight, precision=HIGH
    ) * silu_slope(mixed)
    mixed_wide = extended(grad_mixed.astype(jnp.bfloat16), (("sites", 2),), 1).astype(
        grad_mixed.dtype
    )
    mix_terms = []
    grad_pooled = jnp.zeros(pooled.shape, jnp.float32)
    for shift_by in (-1, 0, 1):
        mix_terms.append(
            jnp.einsum(
                "sct,sot->co",
                pooled_wide[:, :, 1 + shift_by : 1 + shift_by + local],
                grad_mixed,
                precision=HIGH,
            )
        )
        grad_pooled = grad_pooled + jnp.einsum(
            "co,sot->sct",
            mix_weight[shift_by + 1],
            mixed_wide[:, :, 1 - shift_by : 1 - shift_by + local],
            precision=HIGH,
        )
    grad_pre = (grad_pooled / haps)[:, None] * silu_slope(pre)
    term_conv = jnp.einsum("shtk,shct->kc", patches, grad_pre, precision=HIGH)
    term_bias = jnp.sum(grad_pre, axis=(0, 1, 3))
    small = (term_conv, term_bias, jnp.stack(mix_terms), term_embed, term_gain)
    flat_small = jnp.concatenate([t.reshape(-1) for t in small])
    grad_attention, flat_small = butterfly_sum(flat_terms, flat_small)
    pieces = []
    lower = 0
    for t in small:
        pieces.append(flat_small[lower : lower + t.size].reshape(t.shape))
        lower += t.size
    grad_conv, grad_bias, grad_mix, grad_embed, grad_gain = pieces
    return (grad_attention, grad_conv, grad_bias, grad_mix, grad_embed, grad_gain)


def solution(mesh):
    placed = (
        P("sims", None, "sites"),
        P("sims", "sites"),
        P("sims"),
        P("sims", "sites", None),
        P(),
        P(),
        P(),
        P(),
        P(),
        P(),
    )
    return jax.shard_map(
        per_device,
        mesh=mesh,
        in_specs=placed,
        out_specs=(P(("sims", "sites")), P(), P(), P(), P(), P()),
        check_vma=False,
    )
```

```python
import functools

import jax
import jax.numpy as jnp
from jax import lax
from jax.experimental import pallas as pl
from jax.experimental.pallas import tpu as pltpu
from jax.sharding import PartitionSpec as P

HEADS = 8
HEAD_DIM = 64
BAND = 512


HIGH = lax.Precision.HIGHEST
EPS = 1e-06


def extended(cells, sides, width):
    for axis, dim in sides:
        count = lax.axis_size(axis)
        head = lax.slice_in_dim(cells, 0, width, axis=dim)
        tail = lax.slice_in_dim(cells, cells.shape[dim] - width, cells.shape[dim], axis=dim)
        cells = jnp.concatenate(
            [
                lax.ppermute(tail, axis, [(i, (i + 1) % count) for i in range(count)]),
                cells,
                lax.ppermute(head, axis, [((i + 1) % count, i) for i in range(count)]),
            ],
            axis=dim,
        )
    return cells


def from_behind(value, axis, steps):
    count = lax.axis_size(axis)
    pairs = [(source, (source + steps) % count) for source in range(count)]
    return lax.ppermute(value, axis, pairs)


def silu_slope(value):
    sigma = jax.nn.sigmoid(value)
    return sigma * (1.0 + value * (1.0 - sigma))


def block_offsets(count, reach_blocks):
    chosen = []
    taken = []
    for distance in range(reach_blocks + 1):
        for offset in (distance, -distance):
            if offset % count not in taken:
                taken.append(offset % count)
                chosen.append(offset)
    return chosen


def split_heads(array, heads):
    return array.reshape(array.shape[0], array.shape[1], heads, array.shape[2] // heads)


def band_scores(query, keys, prior, query_places, key_places, limit, cycle_tokens, factor):
    scores = jnp.einsum("sqhe,skhe->shqk", query, keys, preferred_element_type=jnp.float32) * factor
    scores = scores + prior.astype(jnp.float32)[:, None, None, :]
    apart = (key_places[None, :] - query_places[:, None]) % cycle_tokens
    apart = jnp.minimum(apart, cycle_tokens - apart)
    inside = apart[None, None] <= limit[:, None, None, None]
    return (scores, inside)


def bit_count(size):
    bits = size.bit_length() - 1
    assert 1 << bits == size
    return bits


def butterfly_sum(flat, small):
    sims_bits = bit_count(lax.axis_size("sims"))
    sites_bits = bit_count(lax.axis_size("sites"))
    total_bits = sims_bits + sites_bits
    chunk = flat.shape[0] >> total_bits
    dim_of = {}
    for bit in range(sims_bits):
        dim_of[("sims", bit)] = sims_bits - 1 - bit
    for bit in range(sites_bits):
        dim_of[("sites", bit)] = total_bits - 1 - bit
    order = [("sims", 0), ("sims", sims_bits - 1)]
    pending = [("sims", b) for b in range(1, sims_bits - 1)]
    pending_sites = [("sites", b) for b in (2, 3, 0, 1) if b < sites_bits]
    pending_sites += [("sites", b) for b in range(sites_bits) if ("sites", b) not in pending_sites]
    while pending or pending_sites:
        if pending:
            order.append(pending.pop(0))
        if pending_sites:
            order.append(pending_sites.pop(0))
    order = list(dict.fromkeys(order))
    cells = flat.reshape((2,) * total_bits + (chunk // LANES, LANES))
    cells = cells.transpose([dim_of[o] for o in order] + [total_bits, total_bits + 1])
    current = cells.reshape(-1, LANES)
    small_order = order[3:4] + order[2:3] + order[1:2] + order[0:1] + order[5:6] + order[4:5]
    small_order += order[8:9] + order[6:7] + order[7:8]
    small_order += [o for o in order if o not in small_order]
    small_order = list(dict.fromkeys(small_order))
    return butterfly_kernel(current, small, order, small_order, chunk)


LANES = 256


def butterfly_body(order, small_order, steps_rows, small_rows, big_ref, small_ref, out_ref, small_out_ref,
                   acc, small_acc, recv, small_recv, send_sems, recv_sems, small_send_sems,
                   small_recv_sems):
    me = {"sims": lax.axis_index("sims"), "sites": lax.axis_index("sites")}
    def partner(axis, bit):
        step = 1 << bit
        mine = (me[axis] // step) % 2
        other = dict(me)
        other[axis] = me[axis] + (1 - 2 * mine) * step
        return ((other["sims"], other["sites"]), mine)

    partners = [partner(axis, bit) for axis, bit in order]
    small_partners = [partner(axis, bit)[0] for axis, bit in small_order]
    barrier = pltpu.get_barrier_semaphore()
    for device, _ in partners:
        pl.semaphore_signal(barrier, inc=1, device_id=device, device_id_type=pl.DeviceIdType.MESH)
    pl.semaphore_wait(barrier, len(partners))
    acc[...] = big_ref[...]
    small_acc[...] = small_ref[...]
    base = 0
    lower = 0
    for k, ((device, mine), rows) in enumerate(zip(partners, steps_rows)):
        keep = pl.multiple_of(base + mine * rows, 8)
        away = pl.multiple_of(base + (1 - mine) * rows, 8)
        big_copy = pltpu.make_async_remote_copy(
            src_ref=acc.at[pl.ds(away, rows)],
            dst_ref=recv.at[pl.ds(lower, rows)],
            send_sem=send_sems.at[k],
            recv_sem=recv_sems.at[k],
            device_id=device,
            device_id_type=pl.DeviceIdType.MESH,
        )
        small_copy = pltpu.make_async_remote_copy(
            src_ref=small_acc,
            dst_ref=small_recv.at[k],
            send_sem=small_send_sems.at[k],
            recv_sem=small_recv_sems.at[k],
            device_id=small_partners[k],
            device_id_type=pl.DeviceIdType.MESH,
        )
        big_copy.start()
        small_copy.start()
        big_copy.wait_send()
        small_copy.wait_send()
        big_copy.wait_recv()
        small_copy.wait_recv()
        acc[pl.ds(keep, rows)] = acc[pl.ds(keep, rows)] + recv[pl.ds(lower, rows)]
        small_acc[...] = small_acc[...] + small_recv[k]
        base = keep
        lower += rows
    out_ref[...] = acc[pl.ds(pl.multiple_of(base, 8), steps_rows[-1])]
    small_out_ref[...] = small_acc[...]


def butterfly_kernel(current, small, order, small_order, chunk):
    size = small.shape[0]
    small_rows = -(-size // (LANES * 8)) * 8
    small_grid = jnp.pad(small, (0, small_rows * LANES - size)).reshape(small_rows, LANES)
    big_rows = current.shape[0]
    steps_rows = [big_rows >> (k + 1) for k in range(len(order))]
    f32 = jnp.float32
    out, small_out = pl.pallas_call(
        functools.partial(butterfly_body, order, small_order, steps_rows, small_rows),
        out_shape=(
            jax.ShapeDtypeStruct((steps_rows[-1], LANES), f32),
            jax.ShapeDtypeStruct((small_rows, LANES), f32),
        ),
        in_specs=[pl.BlockSpec(memory_space=pltpu.VMEM)] * 2,
        out_specs=(pl.BlockSpec(memory_space=pltpu.VMEM),) * 2,
        scratch_shapes=[
            pltpu.VMEM((big_rows, LANES), f32),
            pltpu.VMEM((small_rows, LANES), f32),
            pltpu.VMEM((sum(steps_rows), LANES), f32),
            pltpu.VMEM((len(order), small_rows, LANES), f32),
            pltpu.SemaphoreType.DMA((len(order),)),
            pltpu.SemaphoreType.DMA((len(order),)),
            pltpu.SemaphoreType.DMA((len(order),)),
            pltpu.SemaphoreType.DMA((len(order),)),
        ],
        compiler_params=pltpu.CompilerParams(
            collective_id=0, has_side_effects=True, vmem_limit_bytes=48 * 1024 * 1024
        ),
    )(current, small_grid)
    return out.reshape(chunk), small_out.reshape(-1)[:size]

def exchange_body(shifts, per_slot, src_ref, out_ref, held, send_sems, recv_sems):
    place = lax.axis_index("sites")
    row = lax.axis_index("sims")
    count = lax.axis_size("sites")
    targets = [(row, lax.rem(place + shift + count, count)) for shift in shifts]
    barrier = pltpu.get_barrier_semaphore()
    for device in targets:
        pl.semaphore_signal(barrier, inc=1, device_id=device, device_id_type=pl.DeviceIdType.MESH)
    pl.semaphore_wait(barrier, len(targets))
    copies = []
    for slot, device in enumerate(targets):
        copy = pltpu.make_async_remote_copy(
            src_ref=src_ref.at[slot] if per_slot else src_ref,
            dst_ref=held.at[slot],
            send_sem=send_sems.at[slot],
            recv_sem=recv_sems.at[slot],
            device_id=device,
            device_id_type=pl.DeviceIdType.MESH,
        )
        copy.start()
        copies.append(copy)
    for copy in copies:
        copy.wait_send()
    for copy in copies:
        copy.wait_recv()
    out_ref[...] = held[...]


def exchange(block, shifts, per_slot, collective):
    slots = len(shifts)
    shape = block.shape[1:] if per_slot else block.shape
    return pl.pallas_call(
        functools.partial(exchange_body, shifts, per_slot),
        out_shape=jax.ShapeDtypeStruct((slots,) + shape, block.dtype),
        in_specs=[pl.BlockSpec(memory_space=pltpu.VMEM)],
        out_specs=pl.BlockSpec(memory_space=pltpu.VMEM),
        scratch_shapes=[
            pltpu.VMEM((slots,) + shape, block.dtype),
            pltpu.SemaphoreType.DMA((slots,)),
            pltpu.SemaphoreType.DMA((slots,)),
        ],
        compiler_params=pltpu.CompilerParams(
            collective_id=collective, has_side_effects=True, vmem_limit_bytes=32 * 1024 * 1024
        ),
    )(block)


def per_device(
    genotypes,
    key_prior,
    band_reach,
    cotangent,
    conv_weight,
    conv_bias,
    mix_weight,
    embed_weight,
    norm_gain,
    attn_weight,
):
    sims, haps, sites = genotypes.shape
    patch = conv_weight.shape[0]
    local = sites // patch
    width = attn_weight.shape[1]
    heads = HEADS
    factor = HEAD_DIM ** (-0.5)
    count = lax.axis_size("sites")
    cycle_tokens = local * count
    place = lax.axis_index("sites")
    ordinal = jnp.arange(local, dtype=jnp.int32)
    patches = genotypes.astype(jnp.float32).reshape(sims, haps, local, patch)
    pre = (
        jnp.einsum("shtk,kc->shct", patches, conv_weight, precision=HIGH)
        + conv_bias[None, None, :, None]
    )
    pooled = jnp.mean(jax.nn.silu(pre), axis=1)
    pooled_wide = extended(pooled, (("sites", 2),), 1)
    mixed = jnp.zeros((sims, mix_weight.shape[2], local), jnp.float32)
    for shift_by in (-1, 0, 1):
        mixed = mixed + jnp.einsum(
            "co,sct->sot",
            mix_weight[shift_by + 1],
            pooled_wide[:, :, 1 + shift_by : 1 + shift_by + local],
            precision=HIGH,
        )
    activated = jax.nn.silu(mixed)
    embedded = jnp.einsum("sct,cd->std", activated, embed_weight, precision=HIGH).astype(
        jnp.bfloat16
    )
    wide = embedded.astype(jnp.float32)
    inverse = lax.rsqrt(jnp.mean(wide * wide, axis=2, keepdims=True) + EPS)
    normed = (wide * inverse * norm_gain).astype(jnp.bfloat16)
    query = jnp.einsum(
        "std,de->ste", normed, attn_weight[0], preferred_element_type=jnp.float32
    ).astype(jnp.bfloat16)
    keys = jnp.einsum(
        "std,de->ste", normed, attn_weight[1], preferred_element_type=jnp.float32
    ).astype(jnp.bfloat16)
    values = jnp.einsum(
        "std,de->ste", normed, attn_weight[2], preferred_element_type=jnp.float32
    ).astype(jnp.bfloat16)
    query_heads = split_heads(query, heads)
    key_heads = split_heads(keys, heads)
    value_heads = split_heads(values, heads)
    reach_blocks = -(-BAND // local)
    offsets = block_offsets(count, reach_blocks)
    packed = jnp.concatenate(
        [keys, values, key_prior[:, :, None]], axis=2
    )
    lane_pad = -packed.shape[2] % 128
    packed = jnp.pad(packed, ((0, 0), (0, 0), (0, lane_pad)))
    arrived = exchange(packed[0], [-offset for offset in offsets[1:]], False, 1)
    packed_cat = jnp.concatenate([packed[0][None], arrived], axis=0).reshape(
        1, len(offsets) * local, packed.shape[2]
    )
    key_cat = split_heads(packed_cat[:, :, :width], heads)
    value_cat = split_heads(packed_cat[:, :, width : 2 * width], heads)
    prior_cat = packed_cat[:, :, 2 * width]
    key_places = jnp.concatenate([(place + offset) % count * local + ordinal for offset in offsets])
    query_places = place * local + ordinal
    scores, inside = band_scores(
        query_heads, key_cat, prior_cat, query_places, key_places, band_reach, cycle_tokens, factor
    )
    row_top = jnp.max(jnp.where(inside, scores, -jnp.inf), axis=-1, keepdims=True)
    lifted = jnp.where(inside, jnp.exp(scores - row_top), 0.0)
    row_total = jnp.sum(lifted, axis=-1, keepdims=True)
    prob = lifted / row_total
    prob_half = prob.astype(jnp.bfloat16)
    attended_full = jnp.einsum(
        "shqk,skhe->sqhe", prob_half, value_cat, preferred_element_type=jnp.float32
    )
    attended = attended_full.astype(jnp.bfloat16).reshape(sims, local, width)
    grad_attended = jnp.einsum(
        "std,ed->ste", cotangent, attn_weight[3], preferred_element_type=jnp.float32
    ).astype(jnp.bfloat16)
    grad_heads = split_heads(grad_attended, heads)
    delta = jnp.einsum("sqhe,sqhe->shq", grad_heads.astype(jnp.float32), attended_full)
    grad_prob = jnp.einsum(
        "sqhe,skhe->shqk", grad_heads, value_cat, preferred_element_type=jnp.float32
    )
    grad_scores = (prob * (grad_prob - delta[..., None]) * factor).astype(jnp.bfloat16)
    grad_query = jnp.einsum(
        "shqk,skhe->sqhe", grad_scores, key_cat, preferred_element_type=jnp.float32
    ).astype(jnp.bfloat16)
    grad_query = grad_query.reshape(sims, local, width)
    key_part = jnp.einsum(
        "shqk,sqhe->skhe", grad_scores, query_heads, preferred_element_type=jnp.float32
    )
    value_part = jnp.einsum(
        "shqk,sqhe->skhe", prob_half, grad_heads, preferred_element_type=jnp.float32
    )
    key_sum = key_part[:, 0:local]
    value_sum = value_part[:, 0:local]
    parts = jnp.concatenate(
        [key_part[0, local:], value_part[0, local:]], axis=1
    ).astype(jnp.bfloat16).reshape(len(offsets) - 1, local, 2 * width)
    back = jnp.sum(exchange(parts, list(offsets[1:]), True, 2).astype(jnp.float32), axis=0)
    key_sum = key_part[0, :local].reshape(local, width) + back[:, :width]
    value_sum = value_part[0, :local].reshape(local, width) + back[:, width:]
    grad_keys = key_sum.astype(jnp.bfloat16).reshape(sims, local, width)
    grad_values = value_sum.astype(jnp.bfloat16).reshape(sims, local, width)
    term_query = jnp.einsum("std,ste->de", normed, grad_query, preferred_element_type=jnp.float32)
    term_keys = jnp.einsum("std,ste->de", normed, grad_keys, preferred_element_type=jnp.float32)
    term_values = jnp.einsum("std,ste->de", normed, grad_values, preferred_element_type=jnp.float32)
    term_output = jnp.einsum("std,ste->de", attended, cotangent, preferred_element_type=jnp.float32)
    flat_terms = jnp.stack([term_query, term_keys, term_values, term_output]).reshape(-1)
    grad_normed = jnp.einsum(
        "ste,de->std", grad_query, attn_weight[0], preferred_element_type=jnp.float32
    )
    grad_normed = grad_normed + jnp.einsum(
        "ste,de->std", grad_keys, attn_weight[1], preferred_element_type=jnp.float32
    )
    grad_normed = grad_normed + jnp.einsum(
        "ste,de->std", grad_values, attn_weight[2], preferred_element_type=jnp.float32
    )
    term_gain = jnp.sum(grad_normed * wide * inverse, axis=(0, 1))
    scaled = grad_normed * norm_gain
    grad_embedded = (
        inverse * scaled - wide * inverse**3 * jnp.sum(scaled * wide, axis=2, keepdims=True) / width
    )
    grad_embedded = grad_embedded + cotangent.astype(jnp.float32)
    term_embed = jnp.einsum("sct,std->cd", activated, grad_embedded, precision=HIGH)
    grad_mixed = jnp.einsum(
        "std,od->sot", grad_embedded, embed_weight, precision=HIGH
    ) * silu_slope(mixed)
    mixed_wide = extended(grad_mixed.astype(jnp.bfloat16), (("sites", 2),), 1).astype(
        grad_mixed.dtype
    )
    mix_terms = []
    grad_pooled = jnp.zeros(pooled.shape, jnp.float32)
    for shift_by in (-1, 0, 1):
        mix_terms.append(
            jnp.einsum(
                "sct,sot->co",
                pooled_wide[:, :, 1 + shift_by : 1 + shift_by + local],
                grad_mixed,
                precision=HIGH,
            )
        )
        grad_pooled = grad_pooled + jnp.einsum(
            "co,sot->sct",
            mix_weight[shift_by + 1],
            mixed_wide[:, :, 1 - shift_by : 1 - shift_by + local],
            precision=HIGH,
        )
    grad_pre = (grad_pooled / haps)[:, None] * silu_slope(pre)
    term_conv = jnp.einsum("shtk,shct->kc", patches, grad_pre, precision=HIGH)
    term_bias = jnp.sum(grad_pre, axis=(0, 1, 3))
    small = (term_conv, term_bias, jnp.stack(mix_terms), term_embed, term_gain)
    flat_small = jnp.concatenate([t.reshape(-1) for t in small])
    grad_attention, flat_small = butterfly_sum(flat_terms, flat_small)
    pieces = []
    lower = 0
    for t in small:
        pieces.append(flat_small[lower : lower + t.size].reshape(t.shape))
        lower += t.size
    grad_conv, grad_bias, grad_mix, grad_embed, grad_gain = pieces
    return (grad_attention, grad_conv, grad_bias, grad_mix, grad_embed, grad_gain)


def solution(mesh):
    placed = (
        P("sims", None, "sites"),
        P("sims", "sites"),
        P("sims"),
        P("sims", "sites", None),
        P(),
        P(),
        P(),
        P(),
        P(),
        P(),
    )
    return jax.shard_map(
        per_device,
        mesh=mesh,
        in_specs=placed,
        out_specs=(P(("sims", "sites")), P(), P(), P(), P(), P()),
        check_vma=False,
    )
```

```python
import functools

import jax
import jax.numpy as jnp
from jax import lax
from jax.experimental import pallas as pl
from jax.experimental.pallas import tpu as pltpu
from jax.sharding import PartitionSpec as P

HEADS = 8
HEAD_DIM = 64
BAND = 512


HIGH = lax.Precision.HIGHEST
EPS = 1e-06


def extended(cells, sides, width):
    for axis, dim in sides:
        count = lax.axis_size(axis)
        head = lax.slice_in_dim(cells, 0, width, axis=dim)
        tail = lax.slice_in_dim(cells, cells.shape[dim] - width, cells.shape[dim], axis=dim)
        cells = jnp.concatenate(
            [
                lax.ppermute(tail, axis, [(i, (i + 1) % count) for i in range(count)]),
                cells,
                lax.ppermute(head, axis, [((i + 1) % count, i) for i in range(count)]),
            ],
            axis=dim,
        )
    return cells


def from_behind(value, axis, steps):
    count = lax.axis_size(axis)
    pairs = [(source, (source + steps) % count) for source in range(count)]
    return lax.ppermute(value, axis, pairs)


def silu_slope(value):
    sigma = jax.nn.sigmoid(value)
    return sigma * (1.0 + value * (1.0 - sigma))


def block_offsets(count, reach_blocks):
    chosen = []
    taken = []
    for distance in range(reach_blocks + 1):
        for offset in (distance, -distance):
            if offset % count not in taken:
                taken.append(offset % count)
                chosen.append(offset)
    return chosen


def split_heads(array, heads):
    return array.reshape(array.shape[0], array.shape[1], heads, array.shape[2] // heads)


def band_scores(query, keys, prior, query_places, key_places, limit, cycle_tokens, factor):
    scores = jnp.einsum("sqhe,skhe->shqk", query, keys, preferred_element_type=jnp.float32) * factor
    scores = scores + prior.astype(jnp.float32)[:, None, None, :]
    apart = (key_places[None, :] - query_places[:, None]) % cycle_tokens
    apart = jnp.minimum(apart, cycle_tokens - apart)
    inside = apart[None, None] <= limit[:, None, None, None]
    return (scores, inside)


def bit_count(size):
    bits = size.bit_length() - 1
    assert 1 << bits == size
    return bits


def butterfly_sum(flat, small):
    sims_bits = bit_count(lax.axis_size("sims"))
    sites_bits = bit_count(lax.axis_size("sites"))
    total_bits = sims_bits + sites_bits
    chunk = flat.shape[0] >> total_bits
    dim_of = {}
    for bit in range(sims_bits):
        dim_of[("sims", bit)] = sims_bits - 1 - bit
    for bit in range(sites_bits):
        dim_of[("sites", bit)] = total_bits - 1 - bit
    order = [("sims", 0), ("sims", sims_bits - 1)]
    pending = [("sims", b) for b in range(1, sims_bits - 1)]
    pending_sites = [("sites", b) for b in (2, 3, 0, 1) if b < sites_bits]
    pending_sites += [("sites", b) for b in range(sites_bits) if ("sites", b) not in pending_sites]
    while pending or pending_sites:
        if pending:
            order.append(pending.pop(0))
        if pending_sites:
            order.append(pending_sites.pop(0))
    order = list(dict.fromkeys(order))
    cells = flat.reshape((2,) * total_bits + (chunk // LANES, LANES))
    cells = cells.transpose([dim_of[o] for o in order] + [total_bits, total_bits + 1])
    current = cells.reshape(-1, LANES)
    small_order = order[3:4] + order[2:3] + order[1:2] + order[0:1] + order[5:6] + order[4:5]
    small_order += order[8:9] + order[6:7] + order[7:8]
    small_order += [o for o in order if o not in small_order]
    small_order = list(dict.fromkeys(small_order))
    return butterfly_kernel(current, small, order, small_order, chunk)


LANES = 256


def butterfly_body(order, small_order, steps_rows, small_rows, big_ref, small_ref, out_ref, small_out_ref,
                   acc, small_acc, recv, small_recv, send_sems, recv_sems, small_send_sems,
                   small_recv_sems):
    me = {"sims": lax.axis_index("sims"), "sites": lax.axis_index("sites")}
    def partner(axis, bit):
        step = 1 << bit
        mine = (me[axis] // step) % 2
        other = dict(me)
        other[axis] = me[axis] + (1 - 2 * mine) * step
        return ((other["sims"], other["sites"]), mine)

    partners = [partner(axis, bit) for axis, bit in order]
    small_partners = [partner(axis, bit)[0] for axis, bit in small_order]
    barrier = pltpu.get_barrier_semaphore()
    for device, _ in partners:
        pl.semaphore_signal(barrier, inc=1, device_id=device, device_id_type=pl.DeviceIdType.MESH)
    pl.semaphore_wait(barrier, len(partners))
    acc[...] = big_ref[...]
    small_acc[...] = small_ref[...]
    base = 0
    lower = 0
    for k, ((device, mine), rows) in enumerate(zip(partners, steps_rows)):
        keep = pl.multiple_of(base + mine * rows, 8)
        away = pl.multiple_of(base + (1 - mine) * rows, 8)
        big_copy = pltpu.make_async_remote_copy(
            src_ref=acc.at[pl.ds(away, rows)],
            dst_ref=recv.at[pl.ds(lower, rows)],
            send_sem=send_sems.at[k],
            recv_sem=recv_sems.at[k],
            device_id=device,
            device_id_type=pl.DeviceIdType.MESH,
        )
        small_copy = pltpu.make_async_remote_copy(
            src_ref=small_acc,
            dst_ref=small_recv.at[k],
            send_sem=small_send_sems.at[k],
            recv_sem=small_recv_sems.at[k],
            device_id=small_partners[k],
            device_id_type=pl.DeviceIdType.MESH,
        )
        big_copy.start()
        small_copy.start()
        big_copy.wait_send()
        small_copy.wait_send()
        big_copy.wait_recv()
        small_copy.wait_recv()
        acc[pl.ds(keep, rows)] = acc[pl.ds(keep, rows)] + recv[pl.ds(lower, rows)]
        small_acc[...] = small_acc[...] + small_recv[k]
        base = keep
        lower += rows
    out_ref[...] = acc[pl.ds(pl.multiple_of(base, 8), steps_rows[-1])]
    small_out_ref[...] = small_acc[...]


def butterfly_kernel(current, small, order, small_order, chunk):
    size = small.shape[0]
    small_rows = -(-size // (LANES * 8)) * 8
    small_grid = jnp.pad(small, (0, small_rows * LANES - size)).reshape(small_rows, LANES)
    big_rows = current.shape[0]
    steps_rows = [big_rows >> (k + 1) for k in range(len(order))]
    f32 = jnp.float32
    out, small_out = pl.pallas_call(
        functools.partial(butterfly_body, order, small_order, steps_rows, small_rows),
        out_shape=(
            jax.ShapeDtypeStruct((steps_rows[-1], LANES), f32),
            jax.ShapeDtypeStruct((small_rows, LANES), f32),
        ),
        in_specs=[pl.BlockSpec(memory_space=pltpu.VMEM)] * 2,
        out_specs=(pl.BlockSpec(memory_space=pltpu.VMEM),) * 2,
        scratch_shapes=[
            pltpu.VMEM((big_rows, LANES), f32),
            pltpu.VMEM((small_rows, LANES), f32),
            pltpu.VMEM((sum(steps_rows), LANES), f32),
            pltpu.VMEM((len(order), small_rows, LANES), f32),
            pltpu.SemaphoreType.DMA((len(order),)),
            pltpu.SemaphoreType.DMA((len(order),)),
            pltpu.SemaphoreType.DMA((len(order),)),
            pltpu.SemaphoreType.DMA((len(order),)),
        ],
        compiler_params=pltpu.CompilerParams(
            collective_id=0, has_side_effects=True, vmem_limit_bytes=48 * 1024 * 1024
        ),
    )(current, small_grid)
    return out.reshape(chunk), small_out.reshape(-1)[:size]

def exchange_body(shifts, per_slot, src_ref, out_ref, held, send_sems, recv_sems):
    place = lax.axis_index("sites")
    row = lax.axis_index("sims")
    count = lax.axis_size("sites")
    targets = [(row, lax.rem(place + shift + count, count)) for shift in shifts]
    barrier = pltpu.get_barrier_semaphore()
    for device in targets:
        pl.semaphore_signal(barrier, inc=1, device_id=device, device_id_type=pl.DeviceIdType.MESH)
    pl.semaphore_wait(barrier, len(targets))
    copies = []
    for slot, device in enumerate(targets):
        copy = pltpu.make_async_remote_copy(
            src_ref=src_ref.at[slot] if per_slot else src_ref,
            dst_ref=held.at[slot],
            send_sem=send_sems.at[slot],
            recv_sem=recv_sems.at[slot],
            device_id=device,
            device_id_type=pl.DeviceIdType.MESH,
        )
        copy.start()
        copies.append(copy)
    for copy in copies:
        copy.wait_send()
    for copy in copies:
        copy.wait_recv()
    out_ref[...] = held[...]


def exchange(block, shifts, per_slot, collective):
    slots = len(shifts)
    shape = block.shape[1:] if per_slot else block.shape
    return pl.pallas_call(
        functools.partial(exchange_body, shifts, per_slot),
        out_shape=jax.ShapeDtypeStruct((slots,) + shape, block.dtype),
        in_specs=[pl.BlockSpec(memory_space=pltpu.VMEM)],
        out_specs=pl.BlockSpec(memory_space=pltpu.VMEM),
        scratch_shapes=[
            pltpu.VMEM((slots,) + shape, block.dtype),
            pltpu.SemaphoreType.DMA((slots,)),
            pltpu.SemaphoreType.DMA((slots,)),
        ],
        compiler_params=pltpu.CompilerParams(
            collective_id=collective, has_side_effects=True, vmem_limit_bytes=32 * 1024 * 1024
        ),
    )(block)


def per_device(
    genotypes,
    key_prior,
    band_reach,
    cotangent,
    conv_weight,
    conv_bias,
    mix_weight,
    embed_weight,
    norm_gain,
    attn_weight,
):
    sims, haps, sites = genotypes.shape
    patch = conv_weight.shape[0]
    local = sites // patch
    width = attn_weight.shape[1]
    heads = HEADS
    factor = HEAD_DIM ** (-0.5)
    count = lax.axis_size("sites")
    cycle_tokens = local * count
    place = lax.axis_index("sites")
    ordinal = jnp.arange(local, dtype=jnp.int32)
    patches = genotypes.astype(jnp.float32).reshape(sims, haps, local, patch)
    pre = (
        jnp.einsum("shtk,kc->shct", patches, conv_weight, precision=HIGH)
        + conv_bias[None, None, :, None]
    )
    pooled = jnp.mean(jax.nn.silu(pre), axis=1)
    pooled_wide = extended(pooled, (("sites", 2),), 1)
    mixed = jnp.zeros((sims, mix_weight.shape[2], local), jnp.float32)
    for shift_by in (-1, 0, 1):
        mixed = mixed + jnp.einsum(
            "co,sct->sot",
            mix_weight[shift_by + 1],
            pooled_wide[:, :, 1 + shift_by : 1 + shift_by + local],
            precision=HIGH,
        )
    activated = jax.nn.silu(mixed)
    embedded = jnp.einsum("sct,cd->std", activated, embed_weight, precision=HIGH).astype(
        jnp.bfloat16
    )
    wide = embedded.astype(jnp.float32)
    inverse = lax.rsqrt(jnp.mean(wide * wide, axis=2, keepdims=True) + EPS)
    normed = (wide * inverse * norm_gain).astype(jnp.bfloat16)
    query = jnp.einsum(
        "std,de->ste", normed, attn_weight[0], preferred_element_type=jnp.float32
    ).astype(jnp.bfloat16)
    query_heads = split_heads(query, heads)
    reach_blocks = -(-BAND // local)
    offsets = block_offsets(count, reach_blocks)
    packed = jnp.concatenate([normed, key_prior[:, :, None]], axis=2)
    lane_pad = -packed.shape[2] % 128
    packed = jnp.pad(packed, ((0, 0), (0, 0), (0, lane_pad)))
    arrived = exchange(packed[0], [-offset for offset in offsets[1:]], False, 1)
    packed_cat = jnp.concatenate([packed[0][None], arrived], axis=0).reshape(
        1, len(offsets) * local, packed.shape[2]
    )
    normed_cat = packed_cat[:, :, :width]
    keys_cat = jnp.einsum(
        "std,de->ste", normed_cat, attn_weight[1], preferred_element_type=jnp.float32
    ).astype(jnp.bfloat16)
    values_cat = jnp.einsum(
        "std,de->ste", normed_cat, attn_weight[2], preferred_element_type=jnp.float32
    ).astype(jnp.bfloat16)
    key_cat = split_heads(keys_cat, heads)
    value_cat = split_heads(values_cat, heads)
    prior_cat = packed_cat[:, :, width]
    key_places = jnp.concatenate([(place + offset) % count * local + ordinal for offset in offsets])
    query_places = place * local + ordinal
    scores, inside = band_scores(
        query_heads, key_cat, prior_cat, query_places, key_places, band_reach, cycle_tokens, factor
    )
    row_top = jnp.max(jnp.where(inside, scores, -jnp.inf), axis=-1, keepdims=True)
    lifted = jnp.where(inside, jnp.exp(scores - row_top), 0.0)
    row_total = jnp.sum(lifted, axis=-1, keepdims=True)
    prob = lifted / row_total
    prob_half = prob.astype(jnp.bfloat16)
    attended_full = jnp.einsum(
        "shqk,skhe->sqhe", prob_half, value_cat, preferred_element_type=jnp.float32
    )
    attended = attended_full.astype(jnp.bfloat16).reshape(sims, local, width)
    grad_attended = jnp.einsum(
        "std,ed->ste", cotangent, attn_weight[3], preferred_element_type=jnp.float32
    ).astype(jnp.bfloat16)
    grad_heads = split_heads(grad_attended, heads)
    delta = jnp.einsum("sqhe,sqhe->shq", grad_heads.astype(jnp.float32), attended_full)
    grad_prob = jnp.einsum(
        "sqhe,skhe->shqk", grad_heads, value_cat, preferred_element_type=jnp.float32
    )
    grad_scores = (prob * (grad_prob - delta[..., None]) * factor).astype(jnp.bfloat16)
    grad_query = jnp.einsum(
        "shqk,skhe->sqhe", grad_scores, key_cat, preferred_element_type=jnp.float32
    ).astype(jnp.bfloat16)
    grad_query = grad_query.reshape(sims, local, width)
    key_part = jnp.einsum(
        "shqk,sqhe->skhe", grad_scores, query_heads, preferred_element_type=jnp.float32
    )
    value_part = jnp.einsum(
        "shqk,sqhe->skhe", prob_half, grad_heads, preferred_element_type=jnp.float32
    )
    key_sum = key_part[:, 0:local]
    value_sum = value_part[:, 0:local]
    parts = jnp.concatenate(
        [key_part[0, local:], value_part[0, local:]], axis=1
    ).astype(jnp.bfloat16).reshape(len(offsets) - 1, local, 2 * width)
    back = jnp.sum(exchange(parts, list(offsets[1:]), True, 2).astype(jnp.float32), axis=0)
    key_sum = key_part[0, :local].reshape(local, width) + back[:, :width]
    value_sum = value_part[0, :local].reshape(local, width) + back[:, width:]
    grad_keys = key_sum.astype(jnp.bfloat16).reshape(sims, local, width)
    grad_values = value_sum.astype(jnp.bfloat16).reshape(sims, local, width)
    term_query = jnp.einsum("std,ste->de", normed, grad_query, preferred_element_type=jnp.float32)
    term_keys = jnp.einsum("std,ste->de", normed, grad_keys, preferred_element_type=jnp.float32)
    term_values = jnp.einsum("std,ste->de", normed, grad_values, preferred_element_type=jnp.float32)
    term_output = jnp.einsum("std,ste->de", attended, cotangent, preferred_element_type=jnp.float32)
    flat_terms = jnp.stack([term_query, term_keys, term_values, term_output]).reshape(-1)
    grad_normed = jnp.einsum(
        "ste,de->std", grad_query, attn_weight[0], preferred_element_type=jnp.float32
    )
    grad_normed = grad_normed + jnp.einsum(
        "ste,de->std", grad_keys, attn_weight[1], preferred_element_type=jnp.float32
    )
    grad_normed = grad_normed + jnp.einsum(
        "ste,de->std", grad_values, attn_weight[2], preferred_element_type=jnp.float32
    )
    term_gain = jnp.sum(grad_normed * wide * inverse, axis=(0, 1))
    scaled = grad_normed * norm_gain
    grad_embedded = (
        inverse * scaled - wide * inverse**3 * jnp.sum(scaled * wide, axis=2, keepdims=True) / width
    )
    grad_embedded = grad_embedded + cotangent.astype(jnp.float32)
    term_embed = jnp.einsum("sct,std->cd", activated, grad_embedded, precision=HIGH)
    grad_mixed = jnp.einsum(
        "std,od->sot", grad_embedded, embed_weight, precision=HIGH
    ) * silu_slope(mixed)
    mixed_wide = extended(grad_mixed.astype(jnp.bfloat16), (("sites", 2),), 1).astype(
        grad_mixed.dtype
    )
    mix_terms = []
    grad_pooled = jnp.zeros(pooled.shape, jnp.float32)
    for shift_by in (-1, 0, 1):
        mix_terms.append(
            jnp.einsum(
                "sct,sot->co",
                pooled_wide[:, :, 1 + shift_by : 1 + shift_by + local],
                grad_mixed,
                precision=HIGH,
            )
        )
        grad_pooled = grad_pooled + jnp.einsum(
            "co,sot->sct",
            mix_weight[shift_by + 1],
            mixed_wide[:, :, 1 - shift_by : 1 - shift_by + local],
            precision=HIGH,
        )
    grad_pre = (grad_pooled / haps)[:, None] * silu_slope(pre)
    term_conv = jnp.einsum("shtk,shct->kc", patches, grad_pre, precision=HIGH)
    term_bias = jnp.sum(grad_pre, axis=(0, 1, 3))
    small = (term_conv, term_bias, jnp.stack(mix_terms), term_embed, term_gain)
    flat_small = jnp.concatenate([t.reshape(-1) for t in small])
    grad_attention, flat_small = butterfly_sum(flat_terms, flat_small)
    pieces = []
    lower = 0
    for t in small:
        pieces.append(flat_small[lower : lower + t.size].reshape(t.shape))
        lower += t.size
    grad_conv, grad_bias, grad_mix, grad_embed, grad_gain = pieces
    return (grad_attention, grad_conv, grad_bias, grad_mix, grad_embed, grad_gain)


def solution(mesh):
    placed = (
        P("sims", None, "sites"),
        P("sims", "sites"),
        P("sims"),
        P("sims", "sites", None),
        P(),
        P(),
        P(),
        P(),
        P(),
        P(),
    )
    return jax.shard_map(
        per_device,
        mesh=mesh,
        in_specs=placed,
        out_specs=(P(("sims", "sites")), P(), P(), P(), P(), P()),
        check_vma=False,
    )
```

```python
import functools

import jax
import jax.numpy as jnp
from jax import lax
from jax.experimental import pallas as pl
from jax.experimental.pallas import tpu as pltpu
from jax.sharding import PartitionSpec as P

HEADS = 8
HEAD_DIM = 64
BAND = 512


HIGH = lax.Precision.HIGHEST
EPS = 1e-06


def extended(cells, sides, width):
    for axis, dim in sides:
        count = lax.axis_size(axis)
        head = lax.slice_in_dim(cells, 0, width, axis=dim)
        tail = lax.slice_in_dim(cells, cells.shape[dim] - width, cells.shape[dim], axis=dim)
        cells = jnp.concatenate(
            [
                lax.ppermute(tail, axis, [(i, (i + 1) % count) for i in range(count)]),
                cells,
                lax.ppermute(head, axis, [((i + 1) % count, i) for i in range(count)]),
            ],
            axis=dim,
        )
    return cells


def from_behind(value, axis, steps):
    count = lax.axis_size(axis)
    pairs = [(source, (source + steps) % count) for source in range(count)]
    return lax.ppermute(value, axis, pairs)


def silu_slope(value):
    sigma = jax.nn.sigmoid(value)
    return sigma * (1.0 + value * (1.0 - sigma))


def block_offsets(count, reach_blocks):
    chosen = []
    taken = []
    for distance in range(reach_blocks + 1):
        for offset in (distance, -distance):
            if offset % count not in taken:
                taken.append(offset % count)
                chosen.append(offset)
    return chosen


def split_heads(array, heads):
    return array.reshape(array.shape[0], array.shape[1], heads, array.shape[2] // heads)


def band_scores(query, keys, prior, query_places, key_places, limit, cycle_tokens, factor):
    scores = jnp.einsum("sqhe,skhe->shqk", query, keys, preferred_element_type=jnp.float32) * factor
    scores = scores + prior.astype(jnp.float32)[:, None, None, :]
    apart = (key_places[None, :] - query_places[:, None]) % cycle_tokens
    apart = jnp.minimum(apart, cycle_tokens - apart)
    inside = apart[None, None] <= limit[:, None, None, None]
    return (scores, inside)


def bit_count(size):
    bits = size.bit_length() - 1
    assert 1 << bits == size
    return bits


def butterfly_sum(flat, small):
    sims_bits = bit_count(lax.axis_size("sims"))
    sites_bits = bit_count(lax.axis_size("sites"))
    total_bits = sims_bits + sites_bits
    chunk = flat.shape[0] >> total_bits
    dim_of = {}
    for bit in range(sims_bits):
        dim_of[("sims", bit)] = sims_bits - 1 - bit
    for bit in range(sites_bits):
        dim_of[("sites", bit)] = total_bits - 1 - bit
    order = [("sims", 0), ("sims", sims_bits - 1)]
    pending = [("sims", b) for b in range(1, sims_bits - 1)]
    pending_sites = [("sites", b) for b in (2, 3, 0, 1) if b < sites_bits]
    pending_sites += [("sites", b) for b in range(sites_bits) if ("sites", b) not in pending_sites]
    while pending or pending_sites:
        if pending:
            order.append(pending.pop(0))
        if pending_sites:
            order.append(pending_sites.pop(0))
    order = list(dict.fromkeys(order))
    cells = flat.reshape((2,) * total_bits + (chunk // LANES, LANES))
    cells = cells.transpose([dim_of[o] for o in order] + [total_bits, total_bits + 1])
    current = cells.reshape(-1, LANES)
    small_order = order[3:4] + order[2:3] + order[1:2] + order[0:1] + order[5:6] + order[4:5]
    small_order += order[8:9] + order[6:7] + order[7:8]
    small_order += [o for o in order if o not in small_order]
    small_order = list(dict.fromkeys(small_order))
    return butterfly_kernel(current, small, order, small_order, chunk)


LANES = 256


def butterfly_body(order, small_order, steps_rows, small_rows, big_ref, small_ref, out_ref, small_out_ref,
                   acc, small_acc, recv, small_recv, send_sems, recv_sems, small_send_sems,
                   small_recv_sems):
    me = {"sims": lax.axis_index("sims"), "sites": lax.axis_index("sites")}
    def partner(axis, bit):
        step = 1 << bit
        mine = (me[axis] // step) % 2
        other = dict(me)
        other[axis] = me[axis] + (1 - 2 * mine) * step
        return ((other["sims"], other["sites"]), mine)

    partners = [partner(axis, bit) for axis, bit in order]
    small_partners = [partner(axis, bit)[0] for axis, bit in small_order]
    barrier = pltpu.get_barrier_semaphore()
    for device, _ in partners:
        pl.semaphore_signal(barrier, inc=1, device_id=device, device_id_type=pl.DeviceIdType.MESH)
    pl.semaphore_wait(barrier, len(partners))
    acc[...] = big_ref[...]
    small_acc[...] = small_ref[...]
    base = 0
    lower = 0
    for k, ((device, mine), rows) in enumerate(zip(partners, steps_rows)):
        keep = pl.multiple_of(base + mine * rows, 8)
        away = pl.multiple_of(base + (1 - mine) * rows, 8)
        big_copy = pltpu.make_async_remote_copy(
            src_ref=acc.at[pl.ds(away, rows)],
            dst_ref=recv.at[pl.ds(lower, rows)],
            send_sem=send_sems.at[k],
            recv_sem=recv_sems.at[k],
            device_id=device,
            device_id_type=pl.DeviceIdType.MESH,
        )
        small_copy = pltpu.make_async_remote_copy(
            src_ref=small_acc,
            dst_ref=small_recv.at[k],
            send_sem=small_send_sems.at[k],
            recv_sem=small_recv_sems.at[k],
            device_id=small_partners[k],
            device_id_type=pl.DeviceIdType.MESH,
        )
        big_copy.start()
        small_copy.start()
        big_copy.wait_send()
        small_copy.wait_send()
        big_copy.wait_recv()
        small_copy.wait_recv()
        acc[pl.ds(keep, rows)] = acc[pl.ds(keep, rows)] + recv[pl.ds(lower, rows)]
        small_acc[...] = small_acc[...] + small_recv[k]
        base = keep
        lower += rows
    out_ref[...] = acc[pl.ds(pl.multiple_of(base, 8), steps_rows[-1])]
    small_out_ref[...] = small_acc[...]


def butterfly_kernel(current, small, order, small_order, chunk):
    size = small.shape[0]
    small_rows = -(-size // (LANES * 8)) * 8
    small_grid = jnp.pad(small, (0, small_rows * LANES - size)).reshape(small_rows, LANES)
    big_rows = current.shape[0]
    steps_rows = [big_rows >> (k + 1) for k in range(len(order))]
    f32 = jnp.float32
    out, small_out = pl.pallas_call(
        functools.partial(butterfly_body, order, small_order, steps_rows, small_rows),
        out_shape=(
            jax.ShapeDtypeStruct((steps_rows[-1], LANES), f32),
            jax.ShapeDtypeStruct((small_rows, LANES), f32),
        ),
        in_specs=[pl.BlockSpec(memory_space=pltpu.VMEM)] * 2,
        out_specs=(pl.BlockSpec(memory_space=pltpu.VMEM),) * 2,
        scratch_shapes=[
            pltpu.VMEM((big_rows, LANES), f32),
            pltpu.VMEM((small_rows, LANES), f32),
            pltpu.VMEM((sum(steps_rows), LANES), f32),
            pltpu.VMEM((len(order), small_rows, LANES), f32),
            pltpu.SemaphoreType.DMA((len(order),)),
            pltpu.SemaphoreType.DMA((len(order),)),
            pltpu.SemaphoreType.DMA((len(order),)),
            pltpu.SemaphoreType.DMA((len(order),)),
        ],
        compiler_params=pltpu.CompilerParams(
            collective_id=0, has_side_effects=True, vmem_limit_bytes=48 * 1024 * 1024
        ),
    )(current, small_grid)
    return out.reshape(chunk), small_out.reshape(-1)[:size]

def exchange_body(shifts, per_slot, src_ref, out_ref, held, send_sems, recv_sems):
    place = lax.axis_index("sites")
    row = lax.axis_index("sims")
    count = lax.axis_size("sites")
    targets = [(row, lax.rem(place + shift + count, count)) for shift in shifts]
    barrier = pltpu.get_barrier_semaphore()
    for device in targets:
        pl.semaphore_signal(barrier, inc=1, device_id=device, device_id_type=pl.DeviceIdType.MESH)
    pl.semaphore_wait(barrier, len(targets))
    copies = []
    for slot, device in enumerate(targets):
        copy = pltpu.make_async_remote_copy(
            src_ref=src_ref.at[slot] if per_slot else src_ref,
            dst_ref=held.at[slot],
            send_sem=send_sems.at[slot],
            recv_sem=recv_sems.at[slot],
            device_id=device,
            device_id_type=pl.DeviceIdType.MESH,
        )
        copy.start()
        copies.append(copy)
    for copy in copies:
        copy.wait_send()
    for copy in copies:
        copy.wait_recv()
    out_ref[...] = held[...]


def exchange(block, shifts, per_slot, collective):
    slots = len(shifts)
    shape = block.shape[1:] if per_slot else block.shape
    return pl.pallas_call(
        functools.partial(exchange_body, shifts, per_slot),
        out_shape=jax.ShapeDtypeStruct((slots,) + shape, block.dtype),
        in_specs=[pl.BlockSpec(memory_space=pltpu.VMEM)],
        out_specs=pl.BlockSpec(memory_space=pltpu.VMEM),
        scratch_shapes=[
            pltpu.VMEM((slots,) + shape, block.dtype),
            pltpu.SemaphoreType.DMA((slots,)),
            pltpu.SemaphoreType.DMA((slots,)),
        ],
        compiler_params=pltpu.CompilerParams(
            collective_id=collective, has_side_effects=True, vmem_limit_bytes=32 * 1024 * 1024
        ),
    )(block)


def per_device(
    genotypes,
    key_prior,
    band_reach,
    cotangent,
    conv_weight,
    conv_bias,
    mix_weight,
    embed_weight,
    norm_gain,
    attn_weight,
):
    sims, haps, sites = genotypes.shape
    patch = conv_weight.shape[0]
    local = sites // patch
    width = attn_weight.shape[1]
    heads = HEADS
    factor = HEAD_DIM ** (-0.5)
    count = lax.axis_size("sites")
    cycle_tokens = local * count
    place = lax.axis_index("sites")
    ordinal = jnp.arange(local, dtype=jnp.int32)
    patches = genotypes.astype(jnp.float32).reshape(sims, haps, local, patch)
    pre = (
        jnp.einsum("shtk,kc->shct", patches, conv_weight, precision=HIGH)
        + conv_bias[None, None, :, None]
    )
    pooled = jnp.mean(jax.nn.silu(pre), axis=1)
    pooled_wide = extended(pooled, (("sites", 2),), 1)
    mixed = jnp.zeros((sims, mix_weight.shape[2], local), jnp.float32)
    for shift_by in (-1, 0, 1):
        mixed = mixed + jnp.einsum(
            "co,sct->sot",
            mix_weight[shift_by + 1],
            pooled_wide[:, :, 1 + shift_by : 1 + shift_by + local],
            precision=HIGH,
        )
    activated = jax.nn.silu(mixed)
    embedded = jnp.einsum("sct,cd->std", activated, embed_weight, precision=HIGH).astype(
        jnp.bfloat16
    )
    wide = embedded.astype(jnp.float32)
    inverse = lax.rsqrt(jnp.mean(wide * wide, axis=2, keepdims=True) + EPS)
    normed = (wide * inverse * norm_gain).astype(jnp.bfloat16)
    query = jnp.einsum(
        "std,de->ste", normed, attn_weight[0], preferred_element_type=jnp.float32
    ).astype(jnp.bfloat16)
    query_heads = split_heads(query, heads)
    reach_blocks = -(-BAND // local)
    offsets = block_offsets(count, reach_blocks)
    packed = jnp.concatenate([normed, key_prior[:, :, None]], axis=2)
    lane_pad = -packed.shape[2] % 128
    packed = jnp.pad(packed, ((0, 0), (0, 0), (0, lane_pad)))
    arrived = exchange(packed[0], [-offset for offset in offsets[1:]], False, 1)
    packed_cat = jnp.concatenate([packed[0][None], arrived], axis=0).reshape(
        1, len(offsets) * local, packed.shape[2]
    )
    normed_cat = packed_cat[:, :, :width]
    keys_cat = jnp.einsum(
        "std,de->ste", normed_cat, attn_weight[1], preferred_element_type=jnp.float32
    ).astype(jnp.bfloat16)
    values_cat = jnp.einsum(
        "std,de->ste", normed_cat, attn_weight[2], preferred_element_type=jnp.float32
    ).astype(jnp.bfloat16)
    key_cat = split_heads(keys_cat, heads)
    value_cat = split_heads(values_cat, heads)
    prior_cat = packed_cat[:, :, width]
    key_places = jnp.concatenate([(place + offset) % count * local + ordinal for offset in offsets])
    query_places = place * local + ordinal
    scores, inside = band_scores(
        query_heads, key_cat, prior_cat, query_places, key_places, band_reach, cycle_tokens, factor
    )
    row_top = jnp.max(jnp.where(inside, scores, -jnp.inf), axis=-1, keepdims=True)
    lifted = jnp.where(inside, jnp.exp(scores - row_top), 0.0)
    row_total = jnp.sum(lifted, axis=-1, keepdims=True)
    prob = lifted / row_total
    prob_half = prob.astype(jnp.bfloat16)
    attended_full = jnp.einsum(
        "shqk,skhe->sqhe", prob_half, value_cat, preferred_element_type=jnp.float32
    )
    attended = attended_full.astype(jnp.bfloat16).reshape(sims, local, width)
    grad_attended = jnp.einsum(
        "std,ed->ste", cotangent, attn_weight[3], preferred_element_type=jnp.float32
    ).astype(jnp.bfloat16)
    grad_heads = split_heads(grad_attended, heads)
    delta = jnp.einsum("sqhe,sqhe->shq", grad_heads.astype(jnp.float32), attended_full)
    grad_prob = jnp.einsum(
        "sqhe,skhe->shqk", grad_heads, value_cat, preferred_element_type=jnp.float32
    )
    grad_scores = (prob * (grad_prob - delta[..., None]) * factor).astype(jnp.bfloat16)
    grad_query = jnp.einsum(
        "shqk,skhe->sqhe", grad_scores, key_cat, preferred_element_type=jnp.float32
    ).astype(jnp.bfloat16)
    grad_query = grad_query.reshape(sims, local, width)
    key_part = jnp.einsum(
        "shqk,sqhe->skhe", grad_scores, query_heads, preferred_element_type=jnp.float32
    )
    value_part = jnp.einsum(
        "shqk,sqhe->skhe", prob_half, grad_heads, preferred_element_type=jnp.float32
    )
    key_sum = key_part[:, 0:local]
    value_sum = value_part[:, 0:local]
    key_rows = key_part[0].reshape(len(offsets) * local, width).astype(jnp.bfloat16)
    value_rows = value_part[0].reshape(len(offsets) * local, width).astype(jnp.bfloat16)
    term_query = jnp.einsum("std,ste->de", normed, grad_query, preferred_element_type=jnp.float32)
    term_keys = jnp.einsum("td,te->de", normed_cat[0], key_rows, preferred_element_type=jnp.float32)
    term_values = jnp.einsum("td,te->de", normed_cat[0], value_rows, preferred_element_type=jnp.float32)
    term_output = jnp.einsum("std,ste->de", attended, cotangent, preferred_element_type=jnp.float32)
    flat_terms = jnp.stack([term_query, term_keys, term_values, term_output]).reshape(-1)
    contrib = jnp.einsum("te,de->td", key_rows, attn_weight[1], preferred_element_type=jnp.float32)
    contrib = contrib + jnp.einsum(
        "te,de->td", value_rows, attn_weight[2], preferred_element_type=jnp.float32
    )
    parts = contrib[local:].astype(jnp.bfloat16).reshape(len(offsets) - 1, local, width)
    back = jnp.sum(exchange(parts, list(offsets[1:]), True, 2).astype(jnp.float32), axis=0)
    grad_normed = jnp.einsum(
        "ste,de->std", grad_query, attn_weight[0], preferred_element_type=jnp.float32
    )
    grad_normed = grad_normed + (contrib[:local] + back)[None]
    term_gain = jnp.sum(grad_normed * wide * inverse, axis=(0, 1))
    scaled = grad_normed * norm_gain
    grad_embedded = (
        inverse * scaled - wide * inverse**3 * jnp.sum(scaled * wide, axis=2, keepdims=True) / width
    )
    grad_embedded = grad_embedded + cotangent.astype(jnp.float32)
    term_embed = jnp.einsum("sct,std->cd", activated, grad_embedded, precision=HIGH)
    grad_mixed = jnp.einsum(
        "std,od->sot", grad_embedded, embed_weight, precision=HIGH
    ) * silu_slope(mixed)
    mixed_wide = extended(grad_mixed.astype(jnp.bfloat16), (("sites", 2),), 1).astype(
        grad_mixed.dtype
    )
    mix_terms = []
    grad_pooled = jnp.zeros(pooled.shape, jnp.float32)
    for shift_by in (-1, 0, 1):
        mix_terms.append(
            jnp.einsum(
                "sct,sot->co",
                pooled_wide[:, :, 1 + shift_by : 1 + shift_by + local],
                grad_mixed,
                precision=HIGH,
            )
        )
        grad_pooled = grad_pooled + jnp.einsum(
            "co,sot->sct",
            mix_weight[shift_by + 1],
            mixed_wide[:, :, 1 - shift_by : 1 - shift_by + local],
            precision=HIGH,
        )
    grad_pre = (grad_pooled / haps)[:, None] * silu_slope(pre)
    term_conv = jnp.einsum("shtk,shct->kc", patches, grad_pre, precision=HIGH)
    term_bias = jnp.sum(grad_pre, axis=(0, 1, 3))
    small = (term_conv, term_bias, jnp.stack(mix_terms), term_embed, term_gain)
    flat_small = jnp.concatenate([t.reshape(-1) for t in small])
    grad_attention, flat_small = butterfly_sum(flat_terms, flat_small)
    pieces = []
    lower = 0
    for t in small:
        pieces.append(flat_small[lower : lower + t.size].reshape(t.shape))
        lower += t.size
    grad_conv, grad_bias, grad_mix, grad_embed, grad_gain = pieces
    return (grad_attention, grad_conv, grad_bias, grad_mix, grad_embed, grad_gain)


def solution(mesh):
    placed = (
        P("sims", None, "sites"),
        P("sims", "sites"),
        P("sims"),
        P("sims", "sites", None),
        P(),
        P(),
        P(),
        P(),
        P(),
        P(),
    )
    return jax.shard_map(
        per_device,
        mesh=mesh,
        in_specs=placed,
        out_specs=(P(("sims", "sites")), P(), P(), P(), P(), P()),
        check_vma=False,
    )
```
